128 devices in a mesh: blk: 8 (over z, core), lat: 16 (over x, y).
Axes of the slice: x: 4, y: 4, z: 4, core: 2. Of those that a mesh axis runs over, the one named last changes fastest.
Arguments:
- ice_area: float32 [5, 12, 512, 8192], P(None, None, 'lat', 'blk'), may hold values from 0.05 to 1
- departure_weights: int32 [9, 512, 8192], P(None, 'lat', 'blk'), may hold values from 0 to 4096, as said below
- weld_rate: float32 [512, 8192], P('lat', 'blk'), may hold values from 0.1 to 1
- ice_cover: int32 [512, 8], P('lat', 'blk'), may hold values from 0 to 1, as said below
- wave_ocean: float32 [128, 25, 128, 256], P(('blk', 'lat')), may hold values from 0.02 to 0.5
- ocean_route: int32 [128, 128], P(('blk', 'lat')), may hold values from 0 to 127, each once within a row
Outputs:
- new_area: float32 [5, 12, 512, 8192], P(None, None, 'lat', 'blk')
The draws below stay inside these ranges and needn't reach their ends.
Inputs may be any that keep to these rules, and one draw needn't show every extreme that they name: `departure_weights`: the nine weights of a cell sum to 4096; each off-centre weight is below 410. `ice_cover`: each device's count of ice-covered rows is a multiple of 2, from 2 to 32; in every longitude band the 16 devices' counts are 2, 4, ..., 32 in some order, so a band holds exactly 272 ice-covered blocks. `ocean_route`: each row is a permutation: every ocean device sends one wave block to every ice device.
All inputs are finite; a program needn't handle non-finite values.
Results may differ from the reference program's by a relative error of at most 0.0001.
Values sent between devices are 32-bit elements; how exact they have to be, the bound alone decides.
A program may use at most 192 MiB of HBM per device.

```python
import math
import jax
import jax.numpy as jnp
import numpy as np
from jax import lax

NCAT = 5
NFSD = 12
FREQ = 25
TY = 32
TX = 1024
BANDS = 16
LON_BANDS = 8
NY = 512
NX = 8192
MINI = 256
SLOTS = 2
N_BLK = 8
N_LAT = 16
DEVICES = 128


def draw_departure_weights(key, part):
    side_weights = jax.random.randint(key, (8, NY, NX), 0, 410, dtype=jnp.int32)
    side_weights = side_weights.at[:, 0, 0].set(0)
    centre = 4096 - jnp.sum(side_weights, axis=0, keepdims=True)
    return jnp.concatenate([side_weights[:4], centre, side_weights[4:]], axis=0).astype(jnp.int32)


def draw_ice_cover(key, part):
    order_key, rank_key = jax.random.split(jax.random.fold_in(key, 7))
    ramp = SLOTS * (jnp.arange(BANDS, dtype=jnp.int32) + 1)
    orders = jax.vmap(lambda sub_key: jax.random.permutation(sub_key, BANDS))(jax.random.split(order_key, LON_BANDS))
    counts = ramp[orders]
    ranks = jax.vmap(lambda sub_key: jax.random.permutation(sub_key, TY))(jax.random.split(rank_key, LON_BANDS * BANDS))
    ranks = ranks.reshape(LON_BANDS, BANDS, TY)
    covered = (ranks < counts[:, :, None]).astype(jnp.int32)
    return jnp.transpose(covered, (1, 2, 0)).reshape(NY, LON_BANDS).astype(jnp.int32)


def block_levels(key, shape, cuts, smallest, top_value):
    loudness = 1.0
    for dim, parts in cuts:
        heights = jax.random.uniform(jax.random.fold_in(jax.random.fold_in(key, 6), dim), (parts,), jnp.float32, smallest / len(cuts), top_value / len(cuts))
        loudness = loudness * jnp.repeat(jnp.exp(heights), shape[dim] // parts).reshape((-1,) + (1,) * (len(shape) - 1 - dim))
    return loudness


def setup_inputs(seed: int = 0) -> dict:
    key_of = jax.random.split(jax.random.key(seed), 7)
    ice_area = jnp.clip(0.05 + 0.95 * jax.random.uniform(key_of[0], (NCAT, NFSD, NY, NX), jnp.float32) ** block_levels(key_of[0], (NCAT, NFSD, NY, NX), ((2, 16), (3, 8)), -0.2, 0.2), 0.05, 1.0)
    departure_weights = draw_departure_weights(jax.random.fold_in(key_of[6], 71), 0)
    weld_rate = jnp.clip(jnp.exp(math.log(1.0) - 2.3025851 * jax.random.uniform(key_of[2], (NY, NX), jnp.float32) ** block_levels(key_of[2], (NY, NX), ((0, 16), (1, 8)), -0.2, 0.2)), 0.1, 1.0)
    ice_cover = draw_ice_cover(jax.random.fold_in(key_of[6], 71), 0)
    wave_ocean = jnp.clip(jnp.exp(math.log(0.5) - 3.218876 * jax.random.uniform(key_of[4], (DEVICES, FREQ, DEVICES, MINI), jnp.float32) ** block_levels(key_of[4], (DEVICES, FREQ, DEVICES, MINI), ((0, 128),), -0.2, 0.2)), 0.02, 0.5)
    ocean_route = jax.vmap(lambda own: jax.random.permutation(own, DEVICES))(jax.random.split(key_of[5], DEVICES)).reshape((DEVICES, DEVICES)).astype(jnp.int32)
    return dict(ice_area=ice_area, departure_weights=departure_weights, weld_rate=weld_rate, ice_cover=ice_cover, wave_ocean=wave_ocean, ocean_route=ocean_route)


fracture_step = 0.1


def fsd_tables():
    floe_index = np.arange(NFSD)
    kernel = 0.06 / (1.0 + np.abs(floe_index[:, None] - floe_index[None, :]))
    lower = np.where(floe_index[None, :] < floe_index[:, None], kernel, 0.0)
    diag_table = np.zeros((NFSD, NFSD))
    for index in range(NFSD - 1):
        diag_table[index + 1, index] = 0.06
    diag_table[NFSD - 1, NFSD - 1] = 0.06
    respond = (floe_index[None, :] / (NFSD - 1.0)) * (np.arange(FREQ)[:, None] + 1.0) / FREQ
    thickness = 1.0 / (1.0 + 0.5 * np.arange(NCAT))
    spread = np.where(floe_index[:, None] < floe_index[None, :], 1.0 / np.maximum(floe_index[None, :], 1), 0.0)
    return (jnp.asarray(kernel, jnp.float32), jnp.asarray(lower, jnp.float32), jnp.asarray(diag_table, jnp.float32), jnp.asarray(respond, jnp.float32), jnp.asarray(thickness, jnp.float32), jnp.asarray(spread, jnp.float32))


def rate_of(wave_field):
    respond = fsd_tables()[3]
    return jnp.einsum('fk,frx->krx', respond, wave_field, precision=lax.Precision.HIGHEST)


def column_physics(area_block, wave_rate, weld_field):
    highest = lax.Precision.HIGHEST
    kernel, lower, diag_table, respond, thickness, spread = fsd_tables()
    loss_rate = jnp.einsum('kj,njrx->nkrx', kernel, area_block, precision=highest)
    inner = jnp.einsum('kj,njrx->nkrx', lower, area_block, precision=highest)
    gain = 2.0 * area_block * inner + jnp.einsum('ki,nirx->nkrx', diag_table, area_block * area_block, precision=highest)
    welded = area_block + weld_field[None, None] * (gain - area_block * loss_rate)
    broken = fracture_step * thickness[:, None, None, None] * wave_rate[None] * welded
    return welded - broken + jnp.einsum('jk,nkrx->njrx', spread, broken, precision=highest)


def reference(ice_area, departure_weights, weld_rate, ice_cover, wave_ocean, ocean_route):
    order = jnp.argsort(ocean_route, axis=1).astype(jnp.int32)
    picked = jnp.take_along_axis(wave_ocean, order[:, None, :, None], axis=2)
    wave = jnp.transpose(picked, (1, 2, 0, 3)).reshape(FREQ, N_BLK, N_LAT, TY, TX)
    wave = jnp.transpose(wave, (0, 2, 3, 1, 4)).reshape(FREQ, NY, NX)
    wide = jnp.concatenate([ice_area[..., -1:], ice_area, ice_area[..., :1]], axis=3)
    ghost = wide[:, :, -1:, ::-1]
    bottom = jnp.zeros_like(wide[:, :, :1])
    padded = jnp.concatenate([bottom, wide, ghost], axis=2)
    weight_scale = departure_weights.astype(jnp.float32) / 4096.0
    moved = jnp.zeros(ice_area.shape, jnp.float32)
    for shift_y in range(3):
        for shift_x in range(3):
            moved = moved + weight_scale[3 * shift_y + shift_x] * padded[:, :, shift_y:shift_y + NY, shift_x:shift_x + NX]
    covered = jnp.repeat(ice_cover, TX, axis=1) > 0

    def band_step(block_index, result):
        first_row = (block_index * TY).astype(jnp.int32)
        piece = lax.dynamic_slice_in_dim(moved, first_row, TY, 2)
        wave_piece = lax.dynamic_slice_in_dim(wave, first_row, TY, 1)
        weld_piece = lax.dynamic_slice_in_dim(weld_rate, first_row, TY, 0)
        mask_piece = lax.dynamic_slice_in_dim(covered, first_row, TY, 0)
        worked = column_physics(piece, rate_of(wave_piece), weld_piece)
        return lax.dynamic_update_slice_in_dim(result, jnp.where(mask_piece[None, None], worked, piece), first_row, 2)

    return lax.fori_loop(0, NY // TY, band_step, moved)
```

```python
import jax
import jax.numpy as jnp
from jax import lax
from jax.experimental import pallas as pl
from jax.experimental.pallas import tpu as pltpu
from jax.sharding import PartitionSpec as P

NCAT = 5
NFSD = 12
CATS = NCAT * NFSD
FREQ = 25
ROWS = 32
COLS = 1024
GROUPS = ROWS // 8
TILES = COLS // 128
NBLK = 8
NLAT = 16
PEERS = NBLK * NLAT
MESH = pl.DeviceIdType.MESH
FLAT = 2 * PEERS
FRONT_LIMIT = 34 * 1024 * 1024
BACK_LIMIT = 16 * 1024 * 1024


def vmem_spec():
    return pl.BlockSpec(memory_space=pltpu.VMEM)


def any_spec():
    return pl.BlockSpec(memory_space=pltpu.HBM)


def front_kernel(route_hbm, wave_hbm, ice_hbm, shares_hbm, moved_ref, rate_ref,
                 wave_v, sums_v, send_v, mid_v, turn_v, ice_v, shares_v, weights_v,
                 south_v, north_v, got_south, got_north, west_v, east_v, got_west, got_east, corner_v,
                 west_h, east_h, route_v, route_sem, wave_sem, ice_sem, shares_sem,
                 lat_send, lat_recv, blk_send, blk_recv, send_sem, recv_sem):
    f32 = jnp.float32
    b = lax.axis_index("blk")
    l = lax.axis_index("lat")
    east_b = lax.rem(b + 1, NBLK)
    west_b = lax.rem(b + NBLK - 1, NBLK)
    at_north = l == NLAT - 1
    at_south = l == 0
    inner_north = l < NLAT - 1
    inner_south = l > 0
    up = jnp.minimum(l + 1, NLAT - 1)
    down = jnp.maximum(l - 1, 0)

    parts = 4
    share = PEERS // parts
    wave_copies = [
        pltpu.make_async_copy(
            wave_hbm.at[:, pl.ds(share * i, share), :], wave_v.at[:, pl.ds(share * i, share), :], wave_sem.at[i]
        )
        for i in range(parts)
    ]
    ice_copies = {
        (g, j): pltpu.make_async_copy(
            ice_hbm.at[:, pl.ds(8 * g, 8), pl.ds(128 * j, 128)],
            ice_v.at[j, :, pl.ds(8 + 8 * g, 8), :],
            ice_sem.at[g, j],
        )
        for g in range(GROUPS)
        for j in range(TILES)
    }
    shares_copy = pltpu.make_async_copy(shares_hbm, shares_v, shares_sem)
    route_copy = pltpu.make_async_copy(route_hbm, route_v, route_sem)
    for copy in [route_copy] + wave_copies:
        copy.start()
    for g in (0, 3, 1, 2):
        for j in range(TILES):
            ice_copies[g, j].start()
        if g == 3:
            shares_copy.start()

    barrier = pltpu.get_barrier_semaphore()

    def greet(dev):
        pl.semaphore_signal(barrier, inc=1, device_id=dev, device_id_type=MESH)

    for k in range(1, NLAT):
        greet((b, lax.rem(l + k, NLAT)))
    for k in range(1, NBLK):
        greet((lax.rem(b + k, NBLK), l))
    for side in (east_b, west_b):
        greet((side, lax.rem(l + 1, NLAT)))
        greet((side, lax.rem(l + NLAT - 1, NLAT)))

    for j in range(TILES):
        for first in range(0, CATS, 8):
            size = min(8, CATS - first)
            for spot in (7, 8 + ROWS):
                ice_v[j, pl.ds(first, size), spot, :] = jnp.zeros((size, 128), f32)

    for i in range(parts):
        wave_copies[i].wait()

        def rows(block, carry):
            first = pl.multiple_of(share * i + block * 8, 8)
            for half in range(2):
                lanes = pl.ds(128 * half, 128)
                total = wave_v[0, pl.ds(first, 8), lanes]
                for f in range(1, FREQ):
                    total = total + wave_v[f, pl.ds(first, 8), lanes] * (f + 1.0)
                sums_v[half, pl.ds(first, 8), :] = total
            return carry

        lax.fori_loop(0, share // 8, rows, 0)

    route_copy.wait()
    route = route_v[...]
    place = (jnp.bitwise_and(route, NLAT - 1) * NBLK + jnp.right_shift(route, 4)) * 2
    row = lax.broadcasted_iota(jnp.int32, (FLAT, PEERS), 0)
    ordered = jnp.zeros((FLAT, 128), f32)
    for half in range(2):
        chosen = (row == place + half).astype(f32)
        ordered = ordered + jnp.dot(
            chosen, sums_v[half], precision=lax.Precision.HIGHEST, preferred_element_type=f32
        )
    send_v[...] = ordered

    pl.semaphore_wait(barrier, NLAT - 1 + NBLK - 1 + 4)

    def lat_copy(k):
        peer = lax.rem(l + k, NLAT)
        return pltpu.make_async_remote_copy(
            src_ref=send_v.at[pl.ds(pl.multiple_of(16 * peer, 16), 16), :],
            dst_ref=mid_v.at[pl.ds(pl.multiple_of(16 * l, 16), 16), :],
            send_sem=lat_send.at[k], recv_sem=lat_recv.at[k],
            device_id=(b, peer), device_id_type=MESH,
        )

    for k in range(1, NLAT):
        lat_copy(k).start()
    mine = pl.ds(pl.multiple_of(16 * l, 16), 16)
    mid_v[mine, :] = send_v[mine, :]

    def remote(source, target, sent, got, dev):
        return pltpu.make_async_remote_copy(
            src_ref=source, dst_ref=target, send_sem=send_sem.at[sent], recv_sem=recv_sem.at[got],
            device_id=dev, device_id_type=MESH,
        )

    for g, spot, target in ((0, 8, south_v), (3, 7 + ROWS, north_v)):
        for j in range(TILES):
            ice_copies[g, j].wait()
        for first in range(0, CATS, 8):
            size = min(8, CATS - first)
            for j in range(TILES):
                target[pl.ds(first, size), pl.ds(128 * j, 128)] = ice_v[j, pl.ds(first, size), spot, :]

    to_south = remote(south_v, got_north, 6, 6, (b, down))
    to_north = remote(north_v, got_south, 7, 7, (b, up))
    over = remote(north_v, got_north, 10, 6, (NBLK - 1 - b, l))

    @pl.when(inner_south)
    def _():
        to_south.start()

    @pl.when(inner_north)
    def _():
        to_north.start()

    @pl.when(at_north)
    def _():
        over.start()

    lane = lax.broadcasted_iota(jnp.int32, (8, 128), 1)
    for g in (0, 3, 1, 2):
        if g in (1, 2):
            for j in range(TILES):
                ice_copies[g, j].wait()
        for tile, target, edge in ((0, west_v, 0), (TILES - 1, east_v, 127)):
            held = jnp.zeros((8, 128), f32)
            for cat in range(CATS):
                shift = (cat + 128 - edge) % 128
                column = ice_v[tile, cat, pl.ds(8 + 8 * g, 8), :]
                held = jnp.where(lane == cat, pltpu.roll(column, shift, 1) if shift else column, held)
            target[pl.ds(8 * g, 8), :] = held

    low = pl.ds(0, 8)
    high = pl.ds(ROWS - 8, 8)
    nw_c, ne_c, sw_c, se_c = (corner_v.at[i] for i in range(4))
    to_east = remote(east_v, got_west, 0, 0, (east_b, l))
    to_west = remote(west_v, got_east, 1, 1, (west_b, l))
    to_ne = remote(east_v.at[high], sw_c, 2, 2, (east_b, up))
    to_nw = remote(west_v.at[high], se_c, 3, 3, (west_b, up))
    to_se = remote(east_v.at[low], nw_c, 4, 4, (east_b, down))
    to_sw = remote(west_v.at[low], ne_c, 5, 5, (west_b, down))
    fold_nw = lax.rem(2 * NBLK - b, NBLK)
    fold_ne = lax.rem(2 * NBLK - 2 - b, NBLK)
    nw_home = jnp.logical_and(at_north, fold_nw == b)
    ne_home = jnp.logical_and(at_north, fold_ne == b)
    nw_away = jnp.logical_and(at_north, fold_nw != b)
    ne_away = jnp.logical_and(at_north, fold_ne != b)
    over_nw = remote(west_v.at[high], nw_c, 8, 4, (fold_nw, l))
    over_ne = remote(east_v.at[high], ne_c, 9, 5, (fold_ne, l))
    to_east.start()
    to_west.start()

    @pl.when(inner_north)
    def _():
        to_ne.start()
        to_nw.start()

    @pl.when(inner_south)
    def _():
        to_se.start()
        to_sw.start()

    @pl.when(nw_away)
    def _():
        over_nw.start()

    @pl.when(ne_away)
    def _():
        over_ne.start()

    @pl.when(nw_home)
    def _():
        corner_v[0] = west_v[high, :]

    @pl.when(ne_home)
    def _():
        corner_v[1] = east_v[high, :]

    @pl.when(at_south)
    def _():
        corner_v[2] = jnp.zeros((8, 128), f32)
        corner_v[3] = jnp.zeros((8, 128), f32)

    shares_copy.wait()
    for g in range(GROUPS):
        for t in range(9):
            weight = shares_v[t, pl.ds(8 * g, 8), :].astype(f32) * (1.0 / 4096.0)
            if t % 3 == 2:
                weight = pltpu.roll(weight, 1, 1)
            elif t % 3 == 0:
                weight = pltpu.roll(weight, COLS - 1, 1)
            weights_v[g, t] = weight

    at_first = lane == 0
    at_last = lane == 127
    batch = 6

    def stencil_group(g):
        def stencil(block, carry):
            before = [None] * batch
            held = [None] * batch
            held_right = [None] * batch
            for j in range(TILES + 1):
                if j < TILES:
                    w = [weights_v[g, t, :, pl.ds(128 * j, 128)] for t in range(9)]
                for i in range(batch):
                    cat = block * batch + i
                    if j < TILES:
                        lower = ice_v[j, cat, pl.ds(7 + 8 * g, 8), :]
                        here = ice_v[j, cat, pl.ds(8 + 8 * g, 8), :]
                        upper = ice_v[j, cat, pl.ds(9 + 8 * g, 8), :]
                        centre = w[1] * lower + w[4] * here + w[7] * upper
                        left = w[0] * lower + w[3] * here + w[6] * upper
                        right = w[2] * lower + w[5] * here + w[8] * upper
                        left = pltpu.roll(left, 1, 1)
                        right = pltpu.roll(right, 127, 1)
                    else:
                        right = 0.0
                    if j > 0:
                        moved_ref[cat, pl.ds(8 * g, 8), pl.ds(128 * (j - 1), 128)] = held[i] + jnp.where(
                            at_last, right, held_right[i]
                        )
                    if j < TILES:
                        held[i] = centre + jnp.where(at_first, 0.0 if j == 0 else before[i], left)
                        before[i] = left
                        held_right[i] = right
            return carry

        lax.fori_loop(0, CATS // batch, stencil, 0)

    stencil_group(0)

    for k in range(1, NLAT):
        lat_copy(k).wait_recv()
    for part in range(NBLK):
        for half in range(2):
            for q in range(2):
                turn_v[pl.ds(32 * part + 16 * q + half, 8, stride=2), :] = mid_v[
                    pl.ds(2 * part + half + 128 * q, 8, stride=16), :
                ]

    def blk_copy(k):
        peer = lax.rem(b + k, NBLK)
        return pltpu.make_async_remote_copy(
            src_ref=turn_v.at[pl.ds(pl.multiple_of(32 * peer, 32), 32), :],
            dst_ref=rate_ref.at[pl.ds(pl.multiple_of(32 * b, 32), 32), :],
            send_sem=blk_send.at[k], recv_sem=blk_recv.at[k],
            device_id=(peer, l), device_id_type=MESH,
        )

    for k in range(1, NBLK):
        blk_copy(k).start()
    own = pl.ds(pl.multiple_of(32 * b, 32), 32)
    rate_ref[own, :] = turn_v[own, :]

    for g in (1, 2, 3):
        stencil_group(g)

    to_east.wait()
    to_west.wait()

    @pl.when(inner_north)
    def _():
        to_ne.wait_send()
        to_nw.wait_send()
        to_se.wait_recv()
        to_sw.wait_recv()

    @pl.when(inner_south)
    def _():
        to_se.wait_send()
        to_sw.wait_send()
        to_ne.wait_recv()
        to_nw.wait_recv()

    @pl.when(nw_away)
    def _():
        over_nw.wait()

    @pl.when(ne_away)
    def _():
        over_ne.wait()

    top_west = jnp.where(at_north, corner_v[0, pl.ds(7, 1), :], corner_v[0, pl.ds(0, 1), :])
    top_east = jnp.where(at_north, corner_v[1, pl.ds(7, 1), :], corner_v[1, pl.ds(0, 1), :])
    for source, target, lower, upper, t, spot in (
        (got_west, west_h, corner_v[2, pl.ds(7, 1), :], top_west, 0, 0),
        (got_east, east_h, corner_v[3, pl.ds(7, 1), :], top_east, 2, 127),
    ):
        target[pl.ds(8, ROWS), :] = source[...]
        target[pl.ds(7, 1), :] = lower
        target[pl.ds(8 + ROWS, 1), :] = upper
        tile = pl.ds(0 if spot == 0 else COLS - 128, 128)
        for g in range(GROUPS):
            rows = pl.ds(8 * g, 8)
            total = jnp.zeros((8, 128), f32)
            for dy in range(3):
                weight = shares_v[3 * dy + t, rows, tile].astype(f32) * (1.0 / 4096.0)
                total = total + weight[:, spot : spot + 1] * target[pl.ds(7 + dy + 8 * g, 8), :]
            source[rows, :] = total

    def columns(block, carry):
        for i in range(6):
            cat = block * 6 + i
            for g in range(GROUPS):
                rows = pl.ds(8 * g, 8)
                west = pltpu.roll(got_west[rows, :], jnp.bitwise_and(128 - cat, 127), 1)
                east = pltpu.roll(got_east[rows, :], 127 - cat, 1)
                moved_ref[cat, rows, pl.ds(0, 128)] += jnp.where(at_first, west, 0.0)
                moved_ref[cat, rows, pl.ds(COLS - 128, 128)] += jnp.where(at_last, east, 0.0)
        return carry

    lax.fori_loop(0, CATS // 6, columns, 0)

    @pl.when(inner_south)
    def _():
        to_south.wait_send()
        to_north.wait_recv()

    @pl.when(at_south)
    def _():
        got_south[...] = jnp.zeros_like(got_south)

    @pl.when(inner_north)
    def _():
        to_north.wait_send()
        to_south.wait_recv()

    @pl.when(at_north)
    def _():
        over.wait()
        first = lax.broadcasted_iota(jnp.int32, (128, 128), 0)
        second = lax.broadcasted_iota(jnp.int32, (128, 128), 1)
        mirror = (first + second == 127).astype(f32)
        for j in range(TILES // 2):
            one = pl.ds(128 * j, 128)
            other = pl.ds(128 * (TILES - 1 - j), 128)
            turned = [
                jnp.dot(got_north[:, lanes], mirror, precision=lax.Precision.HIGHEST, preferred_element_type=f32)
                for lanes in (other, one)
            ]
            got_north[:, one] = turned[0]
            got_north[:, other] = turned[1]

    place_x = lax.broadcasted_iota(jnp.int32, (1, COLS), 1)
    for source, t, spot in ((got_south, 0, 0), (got_north, 6, ROWS - 1)):
        weight = [shares_v[t + dx, pl.ds(spot, 1), :].astype(f32) * (1.0 / 4096.0) for dx in range(3)]
        weight[0] = jnp.where(place_x == 0, 0.0, weight[0])
        weight[2] = jnp.where(place_x == COLS - 1, 0.0, weight[2])
        for first in range(0, CATS, 8):
            size = min(8, CATS - first)
            line = source[pl.ds(first, size), :]
            added = weight[1] * line + weight[0] * pltpu.roll(line, 1, 1) + weight[2] * pltpu.roll(line, COLS - 1, 1)
            for j in range(TILES):
                lanes = pl.ds(128 * j, 128)
                moved_ref[pl.ds(first, size), spot, lanes] += added[:, 128 * j : 128 * (j + 1)]

    for k in range(1, NLAT):
        lat_copy(k).wait_send()
    for k in range(1, NBLK):
        blk_copy(k).wait()


def front(route, wave, ice, shares):
    f32 = jnp.float32
    dma = pltpu.SemaphoreType.DMA
    return pl.pallas_call(
        front_kernel,
        name="front",
        out_shape=(pltpu.VMEM((CATS, ROWS, COLS), f32), pltpu.VMEM((FLAT, 128), f32)),
        in_specs=[any_spec()] * 4,
        out_specs=(vmem_spec(), vmem_spec()),
        scratch_shapes=[
            pltpu.VMEM((FREQ, PEERS, 256), f32),
            pltpu.VMEM((2, PEERS, 128), f32),
            pltpu.VMEM((FLAT, 128), f32),
            pltpu.VMEM((FLAT, 128), f32),
            pltpu.VMEM((FLAT, 128), f32),
            pltpu.VMEM((TILES, CATS, ROWS + 16, 128), f32),
            pltpu.VMEM((9, ROWS, COLS), jnp.int32),
            pltpu.VMEM((GROUPS, 9, 8, COLS), f32),
            pltpu.VMEM((CATS, COLS), f32),
            pltpu.VMEM((CATS, COLS), f32),
            pltpu.VMEM((CATS, COLS), f32),
            pltpu.VMEM((CATS, COLS), f32),
            pltpu.VMEM((ROWS, 128), f32),
            pltpu.VMEM((ROWS, 128), f32),
            pltpu.VMEM((ROWS, 128), f32),
            pltpu.VMEM((ROWS, 128), f32),
            pltpu.VMEM((4, 8, 128), f32),
            pltpu.VMEM((ROWS + 16, 128), f32),
            pltpu.VMEM((ROWS + 16, 128), f32),
            pltpu.VMEM((1, PEERS), jnp.int32),
            dma,
            dma((4,)),
            dma((GROUPS, TILES)),
            dma,
            dma((NLAT,)),
            dma((NLAT,)),
            dma((NBLK,)),
            dma((NBLK,)),
            dma((11,)),
            dma((8,)),
        ],
        compiler_params=pltpu.CompilerParams(
            collective_id=0, has_side_effects=True, vmem_limit_bytes=FRONT_LIMIT
        ),
    )(*(pltpu.with_memory_space_constraint(x, pltpu.HBM) for x in (route, wave, ice, shares)))


def physics(area, weld, crack):
    grown = [None] * NFSD
    lost = None
    for k in range(NFSD):
        total = None
        for d in range(1, NFSD):
            below, above = k - d, k + d
            if below >= 0 and above < NFSD:
                term = (area[below] - area[above]) * (1.0 / (1.0 + d))
            elif below >= 0:
                term = area[below] * (1.0 / (1.0 + d))
            elif above < NFSD:
                term = area[above] * (-1.0 / (1.0 + d))
            else:
                continue
            total = term if total is None else total + term
        rate = weld * area[k]
        value = area[k] + rate * total
        if k > 0:
            value = value + lost
        if k < NFSD - 1:
            lost = rate * area[k]
            value = value - lost
        grown[k] = value
    result = [None] * NFSD
    above = None
    for k in range(NFSD - 1, -1, -1):
        scaled = crack * grown[k]
        value = grown[k] - scaled * float(k) if k > 0 else grown[k]
        if above is not None:
            value = value + above
        above = scaled if above is None else above + scaled
        result[k] = value
    return result


def back_kernel(moved_ref, weld_ref, cover_ref, rate_ref, out_hbm, out_v, weld_v, crack_v, out_sem):
    for g in range(GROUPS):
        rows = pl.ds(8 * g, 8)
        mine = lax.broadcasted_iota(jnp.int32, (8, ROWS), 0) + 8 * g == lax.broadcasted_iota(jnp.int32, (8, ROWS), 1)
        listed = jnp.broadcast_to((cover_ref[...] > 0).astype(jnp.float32), (8, ROWS))
        covered = jnp.sum(jnp.where(mine, listed, 0.0), axis=1, keepdims=True)
        weld_v[rows, :] = weld_ref[rows, :] * covered * 0.06
        for j in range(TILES):
            crack_v[rows, pl.ds(128 * j, 128)] = (
                rate_ref[pl.ds(64 * g + j, 8, stride=8), :] * covered * (0.1 / 11.0 / FREQ)
            )

    def out_copy(g):
        rows = pl.ds(8 * g, 8)
        return pltpu.make_async_copy(out_v.at[:, rows, :], out_hbm.at[:, rows, :], out_sem.at[g])

    for g in range(GROUPS):
        rows = pl.ds(8 * g, 8)

        def column(j, carry):
            lanes = pl.ds(pl.multiple_of(128 * j, 128), 128)
            weld = weld_v[rows, lanes]
            crack = crack_v[rows, lanes]
            for n in range(NCAT):
                area = [moved_ref[NFSD * n + k, rows, lanes] for k in range(NFSD)]
                result = physics(area, weld, crack * (1.0 / (1.0 + 0.5 * n)))
                for k in range(NFSD):
                    out_v[NFSD * n + k, rows, lanes] = result[k]
            return carry

        lax.fori_loop(0, TILES, column, 0)
        out_copy(g).start()

    for g in range(GROUPS):
        out_copy(g).wait()


def back(moved, weld, cover, rate):
    f32 = jnp.float32
    return pl.pallas_call(
        back_kernel,
        name="back",
        out_shape=jax.ShapeDtypeStruct((CATS, ROWS, COLS), f32),
        in_specs=[vmem_spec()] * 4,
        out_specs=any_spec(),
        scratch_shapes=[
            pltpu.VMEM((CATS, ROWS, COLS), f32),
            pltpu.VMEM((ROWS, COLS), f32),
            pltpu.VMEM((ROWS, COLS), f32),
            pltpu.SemaphoreType.DMA((GROUPS,)),
        ],
        compiler_params=pltpu.CompilerParams(vmem_limit_bytes=BACK_LIMIT),
    )(moved, weld, cover, rate)


def on_device(ice_area, departure_weights, weld_rate, ice_cover, wave_ocean, ocean_route):
    ice = ice_area.reshape(CATS, ROWS, COLS)
    moved, rate = front(ocean_route, wave_ocean[0], ice, departure_weights)
    out = back(moved, weld_rate, ice_cover.reshape(1, ROWS), rate)
    return out.reshape(ice_area.shape)


def solution(mesh):
    return jax.shard_map(
        on_device,
        mesh=mesh,
        in_specs=(
            P(None, None, "lat", "blk"),
            P(None, "lat", "blk"),
            P("lat", "blk"),
            P("lat", "blk"),
            P(("blk", "lat"), None, None, None),
            P(("blk", "lat"), None),
        ),
        out_specs=P(None, None, "lat", "blk"),
        check_vma=False,
    )
```

```python
import jax
import jax.numpy as jnp
from jax import lax
from jax.experimental import pallas as pl
from jax.experimental.pallas import tpu as pltpu
from jax.sharding import PartitionSpec as P

NCAT = 5
NFSD = 12
CATS = NCAT * NFSD
FREQ = 25
ROWS = 32
COLS = 1024
GROUPS = ROWS // 8
TILES = COLS // 128
NBLK = 8
NLAT = 16
PEERS = NBLK * NLAT
MESH = pl.DeviceIdType.MESH
FLAT = 2 * PEERS
FRONT_LIMIT = 34 * 1024 * 1024
BACK_LIMIT = 16 * 1024 * 1024


def vmem_spec():
    return pl.BlockSpec(memory_space=pltpu.VMEM)


def any_spec():
    return pl.BlockSpec(memory_space=pltpu.HBM)


def covered_rows(cover, g):
    listed = jnp.broadcast_to((cover > 0).astype(jnp.float32), (8, ROWS))
    mine = lax.broadcasted_iota(jnp.int32, (8, ROWS), 0) + 8 * g == lax.broadcasted_iota(jnp.int32, (8, ROWS), 1)
    return jnp.sum(jnp.where(mine, listed, 0.0), axis=1, keepdims=True)


def welded(area, weld):
    grown = [None] * NFSD
    lost = None
    for k in range(NFSD):
        total = None
        for d in range(1, NFSD):
            below, above = k - d, k + d
            if below >= 0 and above < NFSD:
                term = (area[below] - area[above]) * (1.0 / (1.0 + d))
            elif below >= 0:
                term = area[below] * (1.0 / (1.0 + d))
            elif above < NFSD:
                term = area[above] * (-1.0 / (1.0 + d))
            else:
                continue
            total = term if total is None else total + term
        rate = weld * area[k]
        value = area[k] + rate * total
        if k > 0:
            value = value + lost
        if k < NFSD - 1:
            lost = rate * area[k]
            value = value - lost
        grown[k] = value
    return grown


def front_kernel(route_hbm, wave_hbm, ice_hbm, shares_hbm, weld_hbm, cover_hbm, moved_ref, rate_ref,
                 wave_v, sums_v, send_v, mid_v, turn_v, ice_v, shares_v, weights_v,
                 south_v, north_v, got_south, got_north, west_v, east_v, got_west, got_east, corner_v,
                 west_h, east_h, weld_v, cover_v, route_v, weld_sem, route_sem, wave_sem, ice_sem, shares_sem,
                 lat_send, lat_recv, blk_send, blk_recv, send_sem, recv_sem):
    f32 = jnp.float32
    b = lax.axis_index("blk")
    l = lax.axis_index("lat")
    east_b = lax.rem(b + 1, NBLK)
    west_b = lax.rem(b + NBLK - 1, NBLK)
    at_north = l == NLAT - 1
    at_south = l == 0
    inner_north = l < NLAT - 1
    inner_south = l > 0
    up = jnp.minimum(l + 1, NLAT - 1)
    down = jnp.maximum(l - 1, 0)
    ahead = jnp.logical_or(b < NBLK // 2, l // 4 + lax.rem(l, 4) <= 3)
    behind = jnp.logical_not(ahead)

    parts = 4
    share = PEERS // parts
    wave_copies = [
        pltpu.make_async_copy(
            wave_hbm.at[:, pl.ds(share * i, share), :], wave_v.at[:, pl.ds(share * i, share), :], wave_sem.at[i]
        )
        for i in range(parts)
    ]
    def ice_copy(part, j):
        first, size = ((0, 8), (8, ROWS - 16), (ROWS - 8, 8))[part]
        return pltpu.make_async_copy(
            ice_hbm.at[:, pl.ds(first, size), pl.ds(128 * j, 128)],
            ice_v.at[j, :, pl.ds(8 + first, size), :],
            ice_sem.at[part, j],
        )

    shares_copy = pltpu.make_async_copy(shares_hbm, shares_v, shares_sem)
    route_copy = pltpu.make_async_copy(route_hbm, route_v, route_sem)
    weld_copy = pltpu.make_async_copy(weld_hbm, weld_v, weld_sem.at[0])
    cover_copy = pltpu.make_async_copy(cover_hbm, cover_v, weld_sem.at[1])
    for part in (0, 2):
        for j in range(TILES):
            ice_copy(part, j).start()
    for copy in [route_copy] + wave_copies + [shares_copy]:
        copy.start()
    for j in range(TILES):
        ice_copy(1, j).start()
    weld_copy.start()
    cover_copy.start()

    barrier = pltpu.get_barrier_semaphore()

    def greet(dev):
        pl.semaphore_signal(barrier, inc=1, device_id=dev, device_id_type=MESH)

    for k in range(1, NLAT):
        greet((b, lax.rem(l + k, NLAT)))
    for k in range(1, NBLK):
        greet((lax.rem(b + k, NBLK), l))
    for side in (east_b, west_b):
        greet((side, lax.rem(l + 1, NLAT)))
        greet((side, lax.rem(l + NLAT - 1, NLAT)))

    def remote(source, target, sent, got, dev):
        return pltpu.make_async_remote_copy(
            src_ref=source, dst_ref=target, send_sem=send_sem.at[sent], recv_sem=recv_sem.at[got],
            device_id=dev, device_id_type=MESH,
        )

    for part, spot, target in ((0, 8, south_v), (2, 7 + ROWS, north_v)):
        for j in range(TILES):
            ice_copy(part, j).wait()
        for first in range(0, CATS, 8):
            size = min(8, CATS - first)
            for j in range(TILES):
                target[pl.ds(first, size), pl.ds(128 * j, 128)] = ice_v[j, pl.ds(first, size), spot, :]

    to_south = remote(south_v, got_north, 6, 6, (b, down))
    to_north = remote(north_v, got_south, 7, 7, (b, up))
    over = remote(north_v, got_north, 10, 6, (NBLK - 1 - b, l))

    def send_rows():
        pl.semaphore_wait(barrier, NLAT - 1 + NBLK - 1 + 4)

        @pl.when(inner_south)
        def _():
            to_south.start()

        @pl.when(inner_north)
        def _():
            to_north.start()

        @pl.when(at_north)
        def _():
            over.start()

    pl.when(behind)(send_rows)

    for i in range(parts):
        wave_copies[i].wait()

        def rows(block, carry):
            first = pl.multiple_of(share * i + block * 8, 8)
            for half in range(2):
                lanes = pl.ds(128 * half, 128)
                total = wave_v[0, pl.ds(first, 8), lanes]
                for f in range(1, FREQ):
                    total = total + wave_v[f, pl.ds(first, 8), lanes] * (f + 1.0)
                sums_v[half, pl.ds(first, 8), :] = total
            return carry

        lax.fori_loop(0, share // 8, rows, 0)

    route_copy.wait()
    route = route_v[...]
    place = 2 * route
    row = lax.broadcasted_iota(jnp.int32, (FLAT, PEERS), 0)
    ordered = jnp.zeros((FLAT, 128), f32)
    for half in range(2):
        chosen = (row == place + half).astype(f32)
        ordered = ordered + jnp.dot(
            chosen, sums_v[half], precision=lax.Precision.HIGHEST, preferred_element_type=f32
        )
    send_v[...] = ordered

    def blk_copy(k):
        peer = lax.rem(b + k, NBLK)
        return pltpu.make_async_remote_copy(
            src_ref=send_v.at[pl.ds(pl.multiple_of(32 * peer, 32), 32), :],
            dst_ref=mid_v.at[pl.ds(pl.multiple_of(32 * b, 32), 32), :],
            send_sem=blk_send.at[k], recv_sem=blk_recv.at[k],
            device_id=(peer, l), device_id_type=MESH,
        )

    def send_waves():
        for k in range(1, NBLK):
            blk_copy(k).start()

    pl.when(behind)(send_waves)
    own = pl.ds(pl.multiple_of(32 * b, 32), 32)
    mid_v[own, :] = send_v[own, :]

    for j in range(TILES):
        for first in range(0, CATS, 8):
            size = min(8, CATS - first)
            for spot in (7, 8 + ROWS):
                ice_v[j, pl.ds(first, size), spot, :] = jnp.zeros((size, 128), f32)

    lane = lax.broadcasted_iota(jnp.int32, (8, 128), 1)
    for g in (0, 3, 1, 2):
        if g == 1:
            for j in range(TILES):
                ice_copy(1, j).wait()
        for tile, target, edge in ((0, west_v, 0), (TILES - 1, east_v, 127)):
            held = jnp.zeros((8, 128), f32)
            for cat in range(CATS):
                shift = (cat + 128 - edge) % 128
                column = ice_v[tile, cat, pl.ds(8 + 8 * g, 8), :]
                held = jnp.where(lane == cat, pltpu.roll(column, shift, 1) if shift else column, held)
            target[pl.ds(8 * g, 8), :] = held

    low = pl.ds(0, 8)
    high = pl.ds(ROWS - 8, 8)
    nw_c, ne_c, sw_c, se_c = (corner_v.at[i] for i in range(4))
    to_east = remote(east_v, got_west, 0, 0, (east_b, l))
    to_west = remote(west_v, got_east, 1, 1, (west_b, l))
    to_ne = remote(east_v.at[high], sw_c, 2, 2, (east_b, up))
    to_nw = remote(west_v.at[high], se_c, 3, 3, (west_b, up))
    to_se = remote(east_v.at[low], nw_c, 4, 4, (east_b, down))
    to_sw = remote(west_v.at[low], ne_c, 5, 5, (west_b, down))
    fold_nw = lax.rem(2 * NBLK - b, NBLK)
    fold_ne = lax.rem(2 * NBLK - 2 - b, NBLK)
    nw_home = jnp.logical_and(at_north, fold_nw == b)
    ne_home = jnp.logical_and(at_north, fold_ne == b)
    nw_away = jnp.logical_and(at_north, fold_nw != b)
    ne_away = jnp.logical_and(at_north, fold_ne != b)
    over_nw = remote(west_v.at[high], nw_c, 8, 4, (fold_nw, l))
    over_ne = remote(east_v.at[high], ne_c, 9, 5, (fold_ne, l))
    def send_columns():
        to_east.start()
        to_west.start()

        @pl.when(inner_north)
        def _():
            to_ne.start()
            to_nw.start()

        @pl.when(inner_south)
        def _():
            to_se.start()
            to_sw.start()

        @pl.when(nw_away)
        def _():
            over_nw.start()

        @pl.when(ne_away)
        def _():
            over_ne.start()

    pl.when(behind)(send_columns)

    @pl.when(nw_home)
    def _():
        corner_v[0] = west_v[high, :]

    @pl.when(ne_home)
    def _():
        corner_v[1] = east_v[high, :]

    @pl.when(at_south)
    def _():
        corner_v[2] = jnp.zeros((8, 128), f32)
        corner_v[3] = jnp.zeros((8, 128), f32)

    shares_copy.wait()
    for g in range(GROUPS):
        for t in range(9):
            weight = shares_v[t, pl.ds(8 * g, 8), :].astype(f32) * (1.0 / 4096.0)
            if t % 3 == 2:
                weight = pltpu.roll(weight, 1, 1)
            elif t % 3 == 0:
                weight = pltpu.roll(weight, COLS - 1, 1)
            weights_v[g, t] = weight

    @pl.when(ahead)
    def _():
        send_rows()
        send_columns()
        send_waves()

    at_first = lane == 0
    at_last = lane == 127
    batch = 6

    def stencil_group(g):
        def stencil(block, carry):
            before = [None] * batch
            held = [None] * batch
            held_right = [None] * batch
            for j in range(TILES + 1):
                if j < TILES:
                    w = [weights_v[g, t, :, pl.ds(128 * j, 128)] for t in range(9)]
                for i in range(batch):
                    cat = block * batch + i
                    if j < TILES:
                        lower = ice_v[j, cat, pl.ds(7 + 8 * g, 8), :]
                        here = ice_v[j, cat, pl.ds(8 + 8 * g, 8), :]
                        upper = ice_v[j, cat, pl.ds(9 + 8 * g, 8), :]
                        centre = w[1] * lower + w[4] * here + w[7] * upper
                        left = w[0] * lower + w[3] * here + w[6] * upper
                        right = w[2] * lower + w[5] * here + w[8] * upper
                        left = pltpu.roll(left, 1, 1)
                        right = pltpu.roll(right, 127, 1)
                    else:
                        right = 0.0
                    if j > 0:
                        moved_ref[cat, pl.ds(8 * g, 8), pl.ds(128 * (j - 1), 128)] = held[i] + jnp.where(
                            at_last, right, held_right[i]
                        )
                    if j < TILES:
                        held[i] = centre + jnp.where(at_first, 0.0 if j == 0 else before[i], left)
                        before[i] = left
                        held_right[i] = right
            return carry

        lax.fori_loop(0, CATS // batch, stencil, 0)

    stencil_group(0)

    for g in (1, 2, 3):
        stencil_group(g)

    for k in range(1, NBLK):
        blk_copy(k).wait_recv()
    for part in range(NLAT):
        for half in range(2):
            turn_v[pl.ds(16 * part + half, 8, stride=2), :] = mid_v[pl.ds(2 * part + half, 8, stride=32), :]

    def lat_copy(k):
        peer = lax.rem(l + k, NLAT)
        return pltpu.make_async_remote_copy(
            src_ref=turn_v.at[pl.ds(pl.multiple_of(16 * peer, 16), 16), :],
            dst_ref=rate_ref.at[pl.ds(pl.multiple_of(16 * l, 16), 16), :],
            send_sem=lat_send.at[k], recv_sem=lat_recv.at[k],
            device_id=(b, peer), device_id_type=MESH,
        )

    for k in range(1, NLAT):
        lat_copy(k).start()
    mine = pl.ds(pl.multiple_of(16 * l, 16), 16)
    rate_ref[mine, :] = turn_v[mine, :]

    to_east.wait()
    to_west.wait()

    @pl.when(inner_north)
    def _():
        to_ne.wait_send()
        to_nw.wait_send()
        to_se.wait_recv()
        to_sw.wait_recv()

    @pl.when(inner_south)
    def _():
        to_se.wait_send()
        to_sw.wait_send()
        to_ne.wait_recv()
        to_nw.wait_recv()

    @pl.when(nw_away)
    def _():
        over_nw.wait()

    @pl.when(ne_away)
    def _():
        over_ne.wait()

    top_west = jnp.where(at_north, corner_v[0, pl.ds(7, 1), :], corner_v[0, pl.ds(0, 1), :])
    top_east = jnp.where(at_north, corner_v[1, pl.ds(7, 1), :], corner_v[1, pl.ds(0, 1), :])
    for source, target, lower, upper, t, spot in (
        (got_west, west_h, corner_v[2, pl.ds(7, 1), :], top_west, 0, 0),
        (got_east, east_h, corner_v[3, pl.ds(7, 1), :], top_east, 2, 127),
    ):
        target[pl.ds(8, ROWS), :] = source[...]
        target[pl.ds(7, 1), :] = lower
        target[pl.ds(8 + ROWS, 1), :] = upper
        tile = pl.ds(0 if spot == 0 else COLS - 128, 128)
        for g in range(GROUPS):
            rows = pl.ds(8 * g, 8)
            total = jnp.zeros((8, 128), f32)
            for dy in range(3):
                weight = shares_v[3 * dy + t, rows, tile].astype(f32) * (1.0 / 4096.0)
                total = total + weight[:, spot : spot + 1] * target[pl.ds(7 + dy + 8 * g, 8), :]
            source[rows, :] = total

    for g in range(GROUPS):
        rows = pl.ds(8 * g, 8)
        west = got_west[rows, :]
        east = got_east[rows, :]
        for cat in range(CATS):
            first = pltpu.roll(west, 128 - cat, 1) if cat else west
            moved_ref[cat, rows, pl.ds(0, 128)] += jnp.where(at_first, first, 0.0)
            last = pltpu.roll(east, 127 - cat, 1)
            moved_ref[cat, rows, pl.ds(COLS - 128, 128)] += jnp.where(at_last, last, 0.0)

    weld_copy.wait()
    cover_copy.wait()
    for g in range(GROUPS):
        rows = pl.ds(8 * g, 8)
        weld_v[rows, :] = weld_v[rows, :] * (covered_rows(cover_v[...], g) * 0.06)

    def weld_part(part, carry):
        group = part // NCAT
        n = part - NCAT * group
        rows = pl.ds(pl.multiple_of(8 * group, 8), 8)
        for j in range(TILES):
            lanes = pl.ds(128 * j, 128)
            area = [moved_ref[NFSD * n + k, rows, lanes] for k in range(NFSD)]
            grown = welded(area, weld_v[rows, lanes])
            for k in range(NFSD):
                moved_ref[NFSD * n + k, rows, lanes] = grown[k]
        return carry

    lax.fori_loop(NCAT, 3 * NCAT, weld_part, 0)

    @pl.when(inner_south)
    def _():
        to_south.wait_send()
        to_north.wait_recv()

    @pl.when(at_south)
    def _():
        got_south[...] = jnp.zeros_like(got_south)

    @pl.when(inner_north)
    def _():
        to_north.wait_send()
        to_south.wait_recv()

    @pl.when(at_north)
    def _():
        over.wait()
        first = lax.broadcasted_iota(jnp.int32, (128, 128), 0)
        second = lax.broadcasted_iota(jnp.int32, (128, 128), 1)
        mirror = (first + second == 127).astype(f32)
        for j in range(TILES // 2):
            one = pl.ds(128 * j, 128)
            other = pl.ds(128 * (TILES - 1 - j), 128)
            turned = [
                jnp.dot(got_north[:, lanes], mirror, precision=lax.Precision.HIGHEST, preferred_element_type=f32)
                for lanes in (other, one)
            ]
            got_north[:, one] = turned[0]
            got_north[:, other] = turned[1]

    place_x = lax.broadcasted_iota(jnp.int32, (1, COLS), 1)
    for source, t, spot in ((got_south, 0, 0), (got_north, 6, ROWS - 1)):
        weight = [shares_v[t + dx, pl.ds(spot, 1), :].astype(f32) * (1.0 / 4096.0) for dx in range(3)]
        weight[0] = jnp.where(place_x == 0, 0.0, weight[0])
        weight[2] = jnp.where(place_x == COLS - 1, 0.0, weight[2])
        for first in range(0, CATS, 8):
            size = min(8, CATS - first)
            line = source[pl.ds(first, size), :]
            added = weight[1] * line + weight[0] * pltpu.roll(line, 1, 1) + weight[2] * pltpu.roll(line, COLS - 1, 1)
            for j in range(TILES):
                lanes = pl.ds(128 * j, 128)
                moved_ref[pl.ds(first, size), spot, lanes] += added[:, 128 * j : 128 * (j + 1)]

    lax.fori_loop(0, NCAT, weld_part, 0)
    lax.fori_loop(3 * NCAT, 4 * NCAT, weld_part, 0)

    for k in range(1, NBLK):
        blk_copy(k).wait_send()
    for k in range(1, NLAT):
        lat_copy(k).wait()


def front(route, wave, ice, shares, weld, cover):
    f32 = jnp.float32
    dma = pltpu.SemaphoreType.DMA
    return pl.pallas_call(
        front_kernel,
        name="front",
        out_shape=(pltpu.VMEM((CATS, ROWS, COLS), f32), pltpu.VMEM((FLAT, 128), f32)),
        in_specs=[any_spec()] * 6,
        out_specs=(vmem_spec(), vmem_spec()),
        scratch_shapes=[
            pltpu.VMEM((FREQ, PEERS, 256), f32),
            pltpu.VMEM((2, PEERS, 128), f32),
            pltpu.VMEM((FLAT, 128), f32),
            pltpu.VMEM((FLAT, 128), f32),
            pltpu.VMEM((FLAT, 128), f32),
            pltpu.VMEM((TILES, CATS, ROWS + 16, 128), f32),
            pltpu.VMEM((9, ROWS, COLS), jnp.int32),
            pltpu.VMEM((GROUPS, 9, 8, COLS), f32),
            pltpu.VMEM((CATS, COLS), f32),
            pltpu.VMEM((CATS, COLS), f32),
            pltpu.VMEM((CATS, COLS), f32),
            pltpu.VMEM((CATS, COLS), f32),
            pltpu.VMEM((ROWS, 128), f32),
            pltpu.VMEM((ROWS, 128), f32),
            pltpu.VMEM((ROWS, 128), f32),
            pltpu.VMEM((ROWS, 128), f32),
            pltpu.VMEM((4, 8, 128), f32),
            pltpu.VMEM((ROWS + 16, 128), f32),
            pltpu.VMEM((ROWS + 16, 128), f32),
            pltpu.VMEM((ROWS, COLS), f32),
            pltpu.VMEM((1, ROWS), jnp.int32),
            pltpu.VMEM((1, PEERS), jnp.int32),
            dma((2,)),
            dma,
            dma((4,)),
            dma((3, TILES)),
            dma,
            dma((NLAT,)),
            dma((NLAT,)),
            dma((NBLK,)),
            dma((NBLK,)),
            dma((11,)),
            dma((8,)),
        ],
        compiler_params=pltpu.CompilerParams(
            collective_id=0, has_side_effects=True, vmem_limit_bytes=FRONT_LIMIT
        ),
    )(*(pltpu.with_memory_space_constraint(x, pltpu.HBM) for x in (route, wave, ice, shares, weld, cover)))


def cracked(grown, crack):
    result = [None] * NFSD
    above = None
    for k in range(NFSD - 1, -1, -1):
        scaled = crack * grown[k]
        value = grown[k] - scaled * float(k) if k > 0 else grown[k]
        if above is not None:
            value = value + above
        above = scaled if above is None else above + scaled
        result[k] = value
    return result


def back_kernel(welded_ref, cover_ref, rate_ref, out_hbm, out_v, crack_v, out_sem):
    for g in range(GROUPS):
        rows = pl.ds(8 * g, 8)
        covered = covered_rows(cover_ref[...], g)
        for j in range(TILES):
            for half in range(2):
                crack_v[pl.ds(8 * g + 4 * half, 4), pl.ds(128 * j, 128)] = rate_ref[
                    pl.ds(16 * (j // 2) + 4 * g + 2 * half + j % 2, 4, stride=64), :
                ]
        crack_v[rows, :] = crack_v[rows, :] * covered * (0.1 / 11.0 / FREQ)

    def out_copy(part):
        group = part // NCAT
        cats = pl.ds(NFSD * (part - NCAT * group), NFSD)
        rows = pl.ds(pl.multiple_of(8 * group, 8), 8)
        return pltpu.make_async_copy(out_v.at[cats, rows, :], out_hbm.at[cats, rows, :], out_sem.at[part])

    def chunk(part, carry):
        group = part // NCAT
        n = part - NCAT * group
        rows = pl.ds(pl.multiple_of(8 * group, 8), 8)
        thick = 1.0 / (1.0 + 0.5 * jnp.full((8, 128), n, jnp.int32).astype(jnp.float32))
        for j in range(TILES):
            lanes = pl.ds(128 * j, 128)
            grown = [welded_ref[NFSD * n + k, rows, lanes] for k in range(NFSD)]
            result = cracked(grown, crack_v[rows, lanes] * thick)
            for k in range(NFSD):
                out_v[NFSD * n + k, rows, lanes] = result[k]
        out_copy(part).start()
        return carry

    parts = GROUPS * NCAT
    lax.fori_loop(0, parts, chunk, 0)
    for part in range(parts):
        out_copy(part).wait()


def back(grown, cover, rate):
    f32 = jnp.float32
    return pl.pallas_call(
        back_kernel,
        name="back",
        out_shape=jax.ShapeDtypeStruct((CATS, ROWS, COLS), f32),
        in_specs=[vmem_spec()] * 3,
        out_specs=any_spec(),
        scratch_shapes=[
            pltpu.VMEM((CATS, ROWS, COLS), f32),
            pltpu.VMEM((ROWS, COLS), f32),
            pltpu.SemaphoreType.DMA((GROUPS * NCAT,)),
        ],
        compiler_params=pltpu.CompilerParams(vmem_limit_bytes=BACK_LIMIT),
    )(grown, cover, rate)


def on_device(ice_area, departure_weights, weld_rate, ice_cover, wave_ocean, ocean_route):
    ice = ice_area.reshape(CATS, ROWS, COLS)
    cover = ice_cover.reshape(1, ROWS)
    grown, rate = front(ocean_route, wave_ocean[0], ice, departure_weights, weld_rate, cover)
    out = back(grown, cover, rate)
    return out.reshape(ice_area.shape)


def solution(mesh):
    return jax.shard_map(
        on_device,
        mesh=mesh,
        in_specs=(
            P(None, None, "lat", "blk"),
            P(None, "lat", "blk"),
            P("lat", "blk"),
            P("lat", "blk"),
            P(("blk", "lat"), None, None, None),
            P(("blk", "lat"), None),
        ),
        out_specs=P(None, None, "lat", "blk"),
        check_vma=False,
    )
```

```python
import jax
import jax.numpy as jnp
from jax import lax
from jax.experimental import pallas as pl
from jax.experimental.pallas import tpu as pltpu
from jax.sharding import PartitionSpec as P

NCAT = 5
NFSD = 12
CATS = NCAT * NFSD
FREQ = 25
ROWS = 32
COLS = 1024
GROUPS = ROWS // 8
TILES = COLS // 128
NBLK = 8
NLAT = 16
PEERS = NBLK * NLAT
MESH = pl.DeviceIdType.MESH
FLAT = 2 * PEERS
FRONT_LIMIT = 34 * 1024 * 1024
BACK_LIMIT = 16 * 1024 * 1024


def vmem_spec():
    return pl.BlockSpec(memory_space=pltpu.VMEM)


def any_spec():
    return pl.BlockSpec(memory_space=pltpu.HBM)


def covered_rows(cover, g):
    listed = jnp.broadcast_to((cover > 0).astype(jnp.float32), (8, ROWS))
    mine = lax.broadcasted_iota(jnp.int32, (8, ROWS), 0) + 8 * g == lax.broadcasted_iota(jnp.int32, (8, ROWS), 1)
    return jnp.sum(jnp.where(mine, listed, 0.0), axis=1, keepdims=True)


def toeplitz(c, x):
    size = len(x)
    half = size // 2
    odd = all(c.get(d, 0.0) == -c.get(-d, 0.0) for d in range(size))
    if size % 2 or (odd and size <= 6):
        result = []
        for k in range(size):
            total = None
            for d in range(size):
                below, above = k - d, k + d
                if odd and d and below >= 0 and above < size:
                    term = (x[below] - x[above]) * c[d]
                    total = term if total is None else total + term
                    continue
                for j, scale in ((below, c.get(d, 0.0)), (above, c.get(-d, 0.0))):
                    if 0 <= j < size and scale:
                        term = x[j] * scale
                        total = term if total is None else total + term
                    if d == 0:
                        break
            result.append(total)
        return result
    low, high = x[:half], x[half:]
    span = range(1 - half, half)
    both = toeplitz({d: c.get(d, 0.0) for d in span}, [p + q for p, q in zip(low, high)])
    down = toeplitz({d: c.get(d + half, 0.0) - c.get(d, 0.0) for d in span}, low)
    up = toeplitz({d: c.get(d - half, 0.0) - c.get(d, 0.0) for d in span}, high)
    return [p + q for p, q in zip(both, up)] + [p + q for p, q in zip(both, down)]


def welded(area, weld):
    grown = [None] * NFSD
    lost = None
    totals = toeplitz({d: (1.0 if d > 0 else -1.0) / (1.0 + abs(d)) for d in range(1 - NFSD, NFSD) if d}, area)
    for k in range(NFSD):
        total = totals[k]
        rate = weld * area[k]
        value = area[k] + rate * total
        if k > 0:
            value = value + lost
        if k < NFSD - 1:
            lost = rate * area[k]
            value = value - lost
        grown[k] = value
    return grown


def front_kernel(route_hbm, wave_hbm, ice_hbm, shares_hbm, weld_hbm, cover_hbm, moved_ref, rate_ref,
                 wave_v, sums_v, send_v, mid_v, turn_v, ice_v, shares_v, weights_v,
                 south_v, north_v, got_south, got_north, west_v, east_v, got_west, got_east, corner_v,
                 west_h, east_h, weld_v, cover_v, route_v, weld_sem, route_sem, wave_sem, ice_sem, shares_sem,
                 lat_send, lat_recv, blk_send, blk_recv, send_sem, recv_sem):
    f32 = jnp.float32
    b = lax.axis_index("blk")
    l = lax.axis_index("lat")
    east_b = lax.rem(b + 1, NBLK)
    west_b = lax.rem(b + NBLK - 1, NBLK)
    at_north = l == NLAT - 1
    at_south = l == 0
    inner_north = l < NLAT - 1
    inner_south = l > 0
    up = jnp.minimum(l + 1, NLAT - 1)
    down = jnp.maximum(l - 1, 0)
    ahead = jnp.logical_or(b < NBLK // 2, l // 4 + lax.rem(l, 4) <= 3)
    behind = jnp.logical_not(ahead)

    parts = 4
    share = PEERS // parts
    wave_copies = [
        pltpu.make_async_copy(
            wave_hbm.at[:, pl.ds(share * i, share), :], wave_v.at[:, pl.ds(share * i, share), :], wave_sem.at[i]
        )
        for i in range(parts)
    ]
    def ice_copy(part, j):
        first, size = ((0, 8), (8, ROWS - 16), (ROWS - 8, 8))[part]
        return pltpu.make_async_copy(
            ice_hbm.at[:, pl.ds(first, size), pl.ds(128 * j, 128)],
            ice_v.at[j, :, pl.ds(8 + first, size), :],
            ice_sem.at[part, j],
        )

    shares_copy = pltpu.make_async_copy(shares_hbm, shares_v, shares_sem)
    route_copy = pltpu.make_async_copy(route_hbm, route_v, route_sem)
    weld_copy = pltpu.make_async_copy(weld_hbm, weld_v, weld_sem.at[0])
    cover_copy = pltpu.make_async_copy(cover_hbm, cover_v, weld_sem.at[1])
    for part in (0, 2):
        for j in range(TILES):
            ice_copy(part, j).start()
    for copy in [route_copy] + wave_copies + [shares_copy]:
        copy.start()
    for j in range(TILES):
        ice_copy(1, j).start()
    weld_copy.start()
    cover_copy.start()

    barrier = pltpu.get_barrier_semaphore()

    def greet(dev):
        pl.semaphore_signal(barrier, inc=1, device_id=dev, device_id_type=MESH)

    for k in range(1, NLAT):
        greet((b, lax.rem(l + k, NLAT)))
    for k in range(1, NBLK):
        greet((lax.rem(b + k, NBLK), l))
    for side in (east_b, west_b):
        greet((side, lax.rem(l + 1, NLAT)))
        greet((side, lax.rem(l + NLAT - 1, NLAT)))

    def remote(source, target, sent, got, dev):
        return pltpu.make_async_remote_copy(
            src_ref=source, dst_ref=target, send_sem=send_sem.at[sent], recv_sem=recv_sem.at[got],
            device_id=dev, device_id_type=MESH,
        )

    for part, spot, target in ((0, 8, south_v), (2, 7 + ROWS, north_v)):
        for j in range(TILES):
            ice_copy(part, j).wait()
        for first in range(0, CATS, 8):
            size = min(8, CATS - first)
            for j in range(TILES):
                target[pl.ds(first, size), pl.ds(128 * j, 128)] = ice_v[j, pl.ds(first, size), spot, :]

    to_south = remote(south_v, got_north, 6, 6, (b, down))
    to_north = remote(north_v, got_south, 7, 7, (b, up))
    over = remote(north_v, got_north, 10, 6, (NBLK - 1 - b, l))

    def send_rows():
        pl.semaphore_wait(barrier, NLAT - 1 + NBLK - 1 + 4)

        @pl.when(inner_south)
        def _():
            to_south.start()

        @pl.when(inner_north)
        def _():
            to_north.start()

        @pl.when(at_north)
        def _():
            over.start()

    pl.when(behind)(send_rows)

    for i in range(parts):
        wave_copies[i].wait()

        def rows(block, carry):
            first = pl.multiple_of(share * i + block * 8, 8)
            for half in range(2):
                lanes = pl.ds(128 * half, 128)
                total = wave_v[0, pl.ds(first, 8), lanes]
                for f in range(1, FREQ):
                    total = total + wave_v[f, pl.ds(first, 8), lanes] * (f + 1.0)
                sums_v[half, pl.ds(first, 8), :] = total
            return carry

        lax.fori_loop(0, share // 8, rows, 0)

    route_copy.wait()
    route = route_v[...]
    place = 2 * route
    row = lax.broadcasted_iota(jnp.int32, (FLAT, PEERS), 0)
    ordered = jnp.zeros((FLAT, 128), f32)
    for half in range(2):
        chosen = (row == place + half).astype(f32)
        ordered = ordered + jnp.dot(
            chosen, sums_v[half], precision=lax.Precision.HIGHEST, preferred_element_type=f32
        )
    send_v[...] = ordered

    def blk_copy(k):
        peer = lax.rem(b + k, NBLK)
        return pltpu.make_async_remote_copy(
            src_ref=send_v.at[pl.ds(pl.multiple_of(32 * peer, 32), 32), :],
            dst_ref=mid_v.at[pl.ds(pl.multiple_of(32 * b, 32), 32), :],
            send_sem=blk_send.at[k], recv_sem=blk_recv.at[k],
            device_id=(peer, l), device_id_type=MESH,
        )

    def send_waves():
        for k in range(1, NBLK):
            blk_copy(k).start()

    pl.when(behind)(send_waves)
    own = pl.ds(pl.multiple_of(32 * b, 32), 32)
    mid_v[own, :] = send_v[own, :]

    for j in range(TILES):
        for first in range(0, CATS, 8):
            size = min(8, CATS - first)
            for spot in (7, 8 + ROWS):
                ice_v[j, pl.ds(first, size), spot, :] = jnp.zeros((size, 128), f32)

    lane = lax.broadcasted_iota(jnp.int32, (8, 128), 1)
    for g in (0, 3, 1, 2):
        if g == 1:
            for j in range(TILES):
                ice_copy(1, j).wait()
        for tile, target, edge in ((0, west_v, 0), (TILES - 1, east_v, 127)):
            held = jnp.zeros((8, 128), f32)
            for cat in range(CATS):
                shift = (cat + 128 - edge) % 128
                column = ice_v[tile, cat, pl.ds(8 + 8 * g, 8), :]
                held = jnp.where(lane == cat, pltpu.roll(column, shift, 1) if shift else column, held)
            target[pl.ds(8 * g, 8), :] = held

    low = pl.ds(0, 8)
    high = pl.ds(ROWS - 8, 8)
    nw_c, ne_c, sw_c, se_c = (corner_v.at[i] for i in range(4))
    to_east = remote(east_v, got_west, 0, 0, (east_b, l))
    to_west = remote(west_v, got_east, 1, 1, (west_b, l))
    to_ne = remote(east_v.at[high], sw_c, 2, 2, (east_b, up))
    to_nw = remote(west_v.at[high], se_c, 3, 3, (west_b, up))
    to_se = remote(east_v.at[low], nw_c, 4, 4, (east_b, down))
    to_sw = remote(west_v.at[low], ne_c, 5, 5, (west_b, down))
    fold_nw = lax.rem(2 * NBLK - b, NBLK)
    fold_ne = lax.rem(2 * NBLK - 2 - b, NBLK)
    nw_home = jnp.logical_and(at_north, fold_nw == b)
    ne_home = jnp.logical_and(at_north, fold_ne == b)
    nw_away = jnp.logical_and(at_north, fold_nw != b)
    ne_away = jnp.logical_and(at_north, fold_ne != b)
    over_nw = remote(west_v.at[high], nw_c, 8, 4, (fold_nw, l))
    over_ne = remote(east_v.at[high], ne_c, 9, 5, (fold_ne, l))
    def send_columns():
        to_east.start()
        to_west.start()

        @pl.when(inner_north)
        def _():
            to_ne.start()
            to_nw.start()

        @pl.when(inner_south)
        def _():
            to_se.start()
            to_sw.start()

        @pl.when(nw_away)
        def _():
            over_nw.start()

        @pl.when(ne_away)
        def _():
            over_ne.start()

    pl.when(behind)(send_columns)

    @pl.when(nw_home)
    def _():
        corner_v[0] = west_v[high, :]

    @pl.when(ne_home)
    def _():
        corner_v[1] = east_v[high, :]

    @pl.when(at_south)
    def _():
        corner_v[2] = jnp.zeros((8, 128), f32)
        corner_v[3] = jnp.zeros((8, 128), f32)

    shares_copy.wait()
    for g in range(GROUPS):
        for t in range(9):
            weight = shares_v[t, pl.ds(8 * g, 8), :].astype(f32) * (1.0 / 4096.0)
            if t % 3 == 2:
                weight = pltpu.roll(weight, 1, 1)
            elif t % 3 == 0:
                weight = pltpu.roll(weight, COLS - 1, 1)
            weights_v[g, t] = weight

    @pl.when(ahead)
    def _():
        send_rows()
        send_columns()
        send_waves()

    at_first = lane == 0
    at_last = lane == 127
    batch = 10

    def stencil_group(g):
        def stencil(block, carry):
            before = [None] * batch
            held = [None] * batch
            held_right = [None] * batch
            for j in range(TILES + 1):
                if j < TILES:
                    w = [weights_v[g, t, :, pl.ds(128 * j, 128)] for t in range(9)]
                for i in range(batch):
                    cat = block * batch + i
                    if j < TILES:
                        lower = ice_v[j, cat, pl.ds(7 + 8 * g, 8), :]
                        here = ice_v[j, cat, pl.ds(8 + 8 * g, 8), :]
                        upper = ice_v[j, cat, pl.ds(9 + 8 * g, 8), :]
                        centre = w[1] * lower + w[4] * here + w[7] * upper
                        left = w[0] * lower + w[3] * here + w[6] * upper
                        right = w[2] * lower + w[5] * here + w[8] * upper
                        left = pltpu.roll(left, 1, 1)
                        right = pltpu.roll(right, 127, 1)
                    else:
                        right = 0.0
                    if j > 0:
                        moved_ref[cat, pl.ds(8 * g, 8), pl.ds(128 * (j - 1), 128)] = held[i] + jnp.where(
                            at_last, right, held_right[i]
                        )
                    if j < TILES:
                        held[i] = centre + jnp.where(at_first, 0.0 if j == 0 else before[i], left)
                        before[i] = left
                        held_right[i] = right
            return carry

        lax.fori_loop(0, CATS // batch, stencil, 0)

    stencil_group(0)

    for g in (1, 2, 3):
        stencil_group(g)

    for k in range(1, NBLK):
        blk_copy(k).wait_recv()
    for part in range(NLAT):
        for half in range(2):
            turn_v[pl.ds(16 * part + half, 8, stride=2), :] = mid_v[pl.ds(2 * part + half, 8, stride=32), :]

    def lat_copy(k):
        peer = lax.rem(l + k, NLAT)
        return pltpu.make_async_remote_copy(
            src_ref=turn_v.at[pl.ds(pl.multiple_of(16 * peer, 16), 16), :],
            dst_ref=rate_ref.at[pl.ds(pl.multiple_of(16 * l, 16), 16), :],
            send_sem=lat_send.at[k], recv_sem=lat_recv.at[k],
            device_id=(b, peer), device_id_type=MESH,
        )

    for k in range(1, NLAT):
        lat_copy(k).start()
    mine = pl.ds(pl.multiple_of(16 * l, 16), 16)
    rate_ref[mine, :] = turn_v[mine, :]

    to_east.wait()
    to_west.wait()

    @pl.when(inner_north)
    def _():
        to_ne.wait_send()
        to_nw.wait_send()
        to_se.wait_recv()
        to_sw.wait_recv()

    @pl.when(inner_south)
    def _():
        to_se.wait_send()
        to_sw.wait_send()
        to_ne.wait_recv()
        to_nw.wait_recv()

    @pl.when(nw_away)
    def _():
        over_nw.wait()

    @pl.when(ne_away)
    def _():
        over_ne.wait()

    top_west = jnp.where(at_north, corner_v[0, pl.ds(7, 1), :], corner_v[0, pl.ds(0, 1), :])
    top_east = jnp.where(at_north, corner_v[1, pl.ds(7, 1), :], corner_v[1, pl.ds(0, 1), :])
    for source, target, lower, upper, t, spot in (
        (got_west, west_h, corner_v[2, pl.ds(7, 1), :], top_west, 0, 0),
        (got_east, east_h, corner_v[3, pl.ds(7, 1), :], top_east, 2, 127),
    ):
        target[pl.ds(8, ROWS), :] = source[...]
        target[pl.ds(7, 1), :] = lower
        target[pl.ds(8 + ROWS, 1), :] = upper
        tile = pl.ds(0 if spot == 0 else COLS - 128, 128)
        for g in range(GROUPS):
            rows = pl.ds(8 * g, 8)
            total = jnp.zeros((8, 128), f32)
            for dy in range(3):
                weight = shares_v[3 * dy + t, rows, tile].astype(f32) * (1.0 / 4096.0)
                total = total + weight[:, spot : spot + 1] * target[pl.ds(7 + dy + 8 * g, 8), :]
            source[rows, :] = total

    for g in range(GROUPS):
        rows = pl.ds(8 * g, 8)
        west = got_west[rows, :]
        east = got_east[rows, :]
        for cat in range(CATS):
            first = pltpu.roll(west, 128 - cat, 1) if cat else west
            moved_ref[cat, rows, pl.ds(0, 128)] += jnp.where(at_first, first, 0.0)
            last = pltpu.roll(east, 127 - cat, 1)
            moved_ref[cat, rows, pl.ds(COLS - 128, 128)] += jnp.where(at_last, last, 0.0)

    weld_copy.wait()
    cover_copy.wait()
    for g in range(GROUPS):
        rows = pl.ds(8 * g, 8)
        weld_v[rows, :] = weld_v[rows, :] * (covered_rows(cover_v[...], g) * 0.06)

    def weld_part(part, carry):
        group = part // NCAT
        n = part - NCAT * group
        rows = pl.ds(pl.multiple_of(8 * group, 8), 8)
        for j in range(TILES):
            lanes = pl.ds(128 * j, 128)
            area = [moved_ref[NFSD * n + k, rows, lanes] for k in range(NFSD)]
            grown = welded(area, weld_v[rows, lanes])
            for k in range(NFSD):
                moved_ref[NFSD * n + k, rows, lanes] = grown[k]
        return carry

    lax.fori_loop(NCAT, 3 * NCAT, weld_part, 0)

    @pl.when(inner_south)
    def _():
        to_south.wait_send()
        to_north.wait_recv()

    @pl.when(at_south)
    def _():
        got_south[...] = jnp.zeros_like(got_south)

    @pl.when(inner_north)
    def _():
        to_north.wait_send()
        to_south.wait_recv()

    @pl.when(at_north)
    def _():
        over.wait()
        first = lax.broadcasted_iota(jnp.int32, (128, 128), 0)
        second = lax.broadcasted_iota(jnp.int32, (128, 128), 1)
        mirror = (first + second == 127).astype(f32)
        for j in range(TILES // 2):
            one = pl.ds(128 * j, 128)
            other = pl.ds(128 * (TILES - 1 - j), 128)
            turned = [
                jnp.dot(got_north[:, lanes], mirror, precision=lax.Precision.HIGHEST, preferred_element_type=f32)
                for lanes in (other, one)
            ]
            got_north[:, one] = turned[0]
            got_north[:, other] = turned[1]

    place_x = lax.broadcasted_iota(jnp.int32, (1, COLS), 1)
    for source, t, spot in ((got_south, 0, 0), (got_north, 6, ROWS - 1)):
        weight = [shares_v[t + dx, pl.ds(spot, 1), :].astype(f32) * (1.0 / 4096.0) for dx in range(3)]
        weight[0] = jnp.where(place_x == 0, 0.0, weight[0])
        weight[2] = jnp.where(place_x == COLS - 1, 0.0, weight[2])
        for first in range(0, CATS, 8):
            size = min(8, CATS - first)
            line = source[pl.ds(first, size), :]
            added = weight[1] * line + weight[0] * pltpu.roll(line, 1, 1) + weight[2] * pltpu.roll(line, COLS - 1, 1)
            for j in range(TILES):
                lanes = pl.ds(128 * j, 128)
                moved_ref[pl.ds(first, size), spot, lanes] += added[:, 128 * j : 128 * (j + 1)]

    lax.fori_loop(0, NCAT, weld_part, 0)
    lax.fori_loop(3 * NCAT, 4 * NCAT, weld_part, 0)

    for k in range(1, NBLK):
        blk_copy(k).wait_send()
    for k in range(1, NLAT):
        lat_copy(k).wait()


def front(route, wave, ice, shares, weld, cover):
    f32 = jnp.float32
    dma = pltpu.SemaphoreType.DMA
    return pl.pallas_call(
        front_kernel,
        name="front",
        out_shape=(pltpu.VMEM((CATS, ROWS, COLS), f32), pltpu.VMEM((FLAT, 128), f32)),
        in_specs=[any_spec()] * 6,
        out_specs=(vmem_spec(), vmem_spec()),
        scratch_shapes=[
            pltpu.VMEM((FREQ, PEERS, 256), f32),
            pltpu.VMEM((2, PEERS, 128), f32),
            pltpu.VMEM((FLAT, 128), f32),
            pltpu.VMEM((FLAT, 128), f32),
            pltpu.VMEM((FLAT, 128), f32),
            pltpu.VMEM((TILES, CATS, ROWS + 16, 128), f32),
            pltpu.VMEM((9, ROWS, COLS), jnp.int32),
            pltpu.VMEM((GROUPS, 9, 8, COLS), f32),
            pltpu.VMEM((CATS, COLS), f32),
            pltpu.VMEM((CATS, COLS), f32),
            pltpu.VMEM((CATS, COLS), f32),
            pltpu.VMEM((CATS, COLS), f32),
            pltpu.VMEM((ROWS, 128), f32),
            pltpu.VMEM((ROWS, 128), f32),
            pltpu.VMEM((ROWS, 128), f32),
            pltpu.VMEM((ROWS, 128), f32),
            pltpu.VMEM((4, 8, 128), f32),
            pltpu.VMEM((ROWS + 16, 128), f32),
            pltpu.VMEM((ROWS + 16, 128), f32),
            pltpu.VMEM((ROWS, COLS), f32),
            pltpu.VMEM((1, ROWS), jnp.int32),
            pltpu.VMEM((1, PEERS), jnp.int32),
            dma((2,)),
            dma,
            dma((4,)),
            dma((3, TILES)),
            dma,
            dma((NLAT,)),
            dma((NLAT,)),
            dma((NBLK,)),
            dma((NBLK,)),
            dma((11,)),
            dma((8,)),
        ],
        compiler_params=pltpu.CompilerParams(
            collective_id=0, has_side_effects=True, vmem_limit_bytes=FRONT_LIMIT
        ),
    )(*(pltpu.with_memory_space_constraint(x, pltpu.HBM) for x in (route, wave, ice, shares, weld, cover)))


def cracked(grown, crack):
    result = [None] * NFSD
    above = None
    for k in range(NFSD - 1, -1, -1):
        scaled = crack * grown[k]
        value = grown[k] - scaled * float(k) if k > 0 else grown[k]
        if above is not None:
            value = value + above
        above = scaled if above is None else above + scaled
        result[k] = value
    return result


def back_kernel(welded_ref, cover_ref, rate_ref, out_hbm, out_v, crack_v, out_sem):
    for g in range(GROUPS):
        rows = pl.ds(8 * g, 8)
        covered = covered_rows(cover_ref[...], g)
        for j in range(TILES):
            for half in range(2):
                crack_v[pl.ds(8 * g + 4 * half, 4), pl.ds(128 * j, 128)] = rate_ref[
                    pl.ds(16 * (j // 2) + 4 * g + 2 * half + j % 2, 4, stride=64), :
                ]
        crack_v[rows, :] = crack_v[rows, :] * covered * (0.1 / 11.0 / FREQ)

    def out_copy(part):
        group = part // NCAT
        cats = pl.ds(NFSD * (part - NCAT * group), NFSD)
        rows = pl.ds(pl.multiple_of(8 * group, 8), 8)
        return pltpu.make_async_copy(out_v.at[cats, rows, :], out_hbm.at[cats, rows, :], out_sem.at[part])

    def chunk(part, carry):
        group = part // NCAT
        n = part - NCAT * group
        rows = pl.ds(pl.multiple_of(8 * group, 8), 8)
        thick = 1.0 / (1.0 + 0.5 * jnp.full((8, 128), n, jnp.int32).astype(jnp.float32))
        for j in range(TILES):
            lanes = pl.ds(128 * j, 128)
            grown = [welded_ref[NFSD * n + k, rows, lanes] for k in range(NFSD)]
            result = cracked(grown, crack_v[rows, lanes] * thick)
            for k in range(NFSD):
                out_v[NFSD * n + k, rows, lanes] = result[k]
        out_copy(part).start()
        return carry

    parts = GROUPS * NCAT
    lax.fori_loop(0, parts, chunk, 0)
    for part in range(parts):
        out_copy(part).wait()


def back(grown, cover, rate):
    f32 = jnp.float32
    return pl.pallas_call(
        back_kernel,
        name="back",
        out_shape=jax.ShapeDtypeStruct((CATS, ROWS, COLS), f32),
        in_specs=[vmem_spec()] * 3,
        out_specs=any_spec(),
        scratch_shapes=[
            pltpu.VMEM((CATS, ROWS, COLS), f32),
            pltpu.VMEM((ROWS, COLS), f32),
            pltpu.SemaphoreType.DMA((GROUPS * NCAT,)),
        ],
        compiler_params=pltpu.CompilerParams(vmem_limit_bytes=BACK_LIMIT),
    )(grown, cover, rate)


def on_device(ice_area, departure_weights, weld_rate, ice_cover, wave_ocean, ocean_route):
    ice = ice_area.reshape(CATS, ROWS, COLS)
    cover = ice_cover.reshape(1, ROWS)
    grown, rate = front(ocean_route, wave_ocean[0], ice, departure_weights, weld_rate, cover)
    out = back(grown, cover, rate)
    return out.reshape(ice_area.shape)


def solution(mesh):
    return jax.shard_map(
        on_device,
        mesh=mesh,
        in_specs=(
            P(None, None, "lat", "blk"),
            P(None, "lat", "blk"),
            P("lat", "blk"),
            P("lat", "blk"),
            P(("blk", "lat"), None, None, None),
            P(("blk", "lat"), None),
        ),
        out_specs=P(None, None, "lat", "blk"),
        check_vma=False,
    )
```

```python
import jax
import jax.numpy as jnp
from jax import lax
from jax.experimental import pallas as pl
from jax.experimental.pallas import tpu as pltpu
from jax.sharding import PartitionSpec as P

NCAT = 5
NFSD = 12
CATS = NCAT * NFSD
FREQ = 25
ROWS = 32
COLS = 1024
GROUPS = ROWS // 8
TILES = COLS // 128
NBLK = 8
NLAT = 16
PEERS = NBLK * NLAT
MESH = pl.DeviceIdType.MESH
FLAT = 2 * PEERS
FRONT_LIMIT = 34 * 1024 * 1024
BACK_LIMIT = 16 * 1024 * 1024


def vmem_spec():
    return pl.BlockSpec(memory_space=pltpu.VMEM)


def any_spec():
    return pl.BlockSpec(memory_space=pltpu.HBM)


def covered_rows(cover, g):
    listed = jnp.broadcast_to((cover > 0).astype(jnp.float32), (8, ROWS))
    mine = lax.broadcasted_iota(jnp.int32, (8, ROWS), 0) + 8 * g == lax.broadcasted_iota(jnp.int32, (8, ROWS), 1)
    return jnp.sum(jnp.where(mine, listed, 0.0), axis=1, keepdims=True)


def toeplitz(c, x):
    size = len(x)
    half = size // 2
    odd = all(c.get(d, 0.0) == -c.get(-d, 0.0) for d in range(size))
    if size % 2 or (odd and size <= 6):
        result = []
        for k in range(size):
            total = None
            for d in range(size):
                below, above = k - d, k + d
                if odd and d and below >= 0 and above < size:
                    term = (x[below] - x[above]) * c[d]
                    total = term if total is None else total + term
                    continue
                for j, scale in ((below, c.get(d, 0.0)), (above, c.get(-d, 0.0))):
                    if 0 <= j < size and scale:
                        term = x[j] * scale
                        total = term if total is None else total + term
                    if d == 0:
                        break
            result.append(total)
        return result
    low, high = x[:half], x[half:]
    span = range(1 - half, half)
    both = toeplitz({d: c.get(d, 0.0) for d in span}, [p + q for p, q in zip(low, high)])
    down = toeplitz({d: c.get(d + half, 0.0) - c.get(d, 0.0) for d in span}, low)
    up = toeplitz({d: c.get(d - half, 0.0) - c.get(d, 0.0) for d in span}, high)
    return [p + q for p, q in zip(both, up)] + [p + q for p, q in zip(both, down)]


def welded(area, weld):
    grown = [None] * NFSD
    lost = None
    totals = toeplitz({d: (1.0 if d > 0 else -1.0) / (1.0 + abs(d)) for d in range(1 - NFSD, NFSD) if d}, area)
    for k in range(NFSD):
        total = totals[k]
        rate = weld * area[k]
        value = area[k] + rate * total
        if k > 0:
            value = value + lost
        if k < NFSD - 1:
            lost = rate * area[k]
            value = value - lost
        grown[k] = value
    return grown


def front_kernel(route_hbm, wave_hbm, ice_hbm, shares_hbm, weld_hbm, cover_hbm, moved_ref, rate_ref,
                 wave_v, sums_v, send_v, mid_v, turn_v, ice_v, shares_v, weights_v,
                 south_v, north_v, got_south, got_north, west_v, east_v, got_west, got_east, corner_v,
                 west_h, east_h, weld_v, cover_v, route_v, weld_sem, route_sem, wave_sem, ice_sem, shares_sem,
                 lat_send, lat_recv, blk_send, blk_recv, send_sem, recv_sem):
    f32 = jnp.float32
    b = lax.axis_index("blk")
    l = lax.axis_index("lat")
    east_b = lax.rem(b + 1, NBLK)
    west_b = lax.rem(b + NBLK - 1, NBLK)
    at_north = l == NLAT - 1
    at_south = l == 0
    inner_north = l < NLAT - 1
    inner_south = l > 0
    up = jnp.minimum(l + 1, NLAT - 1)
    down = jnp.maximum(l - 1, 0)
    ahead = b < NBLK // 2
    behind = jnp.logical_not(ahead)

    parts = 4
    share = PEERS // parts
    wave_copies = [
        pltpu.make_async_copy(
            wave_hbm.at[:, pl.ds(share * i, share), :], wave_v.at[:, pl.ds(share * i, share), :], wave_sem.at[i]
        )
        for i in range(parts)
    ]
    def ice_copy(part, j):
        first, size = ((0, 8), (8, ROWS - 16), (ROWS - 8, 8))[part]
        return pltpu.make_async_copy(
            ice_hbm.at[:, pl.ds(first, size), pl.ds(128 * j, 128)],
            ice_v.at[j, :, pl.ds(8 + first, size), :],
            ice_sem.at[part, j],
        )

    shares_copy = pltpu.make_async_copy(shares_hbm, shares_v, shares_sem)
    route_copy = pltpu.make_async_copy(route_hbm, route_v, route_sem)
    weld_copy = pltpu.make_async_copy(weld_hbm, weld_v, weld_sem.at[0])
    cover_copy = pltpu.make_async_copy(cover_hbm, cover_v, weld_sem.at[1])
    for part in (0, 2):
        for j in range(TILES):
            ice_copy(part, j).start()
    for copy in [route_copy] + wave_copies + [shares_copy]:
        copy.start()
    for j in range(TILES):
        ice_copy(1, j).start()
    weld_copy.start()
    cover_copy.start()

    barrier = pltpu.get_barrier_semaphore()

    def greet(dev):
        pl.semaphore_signal(barrier, inc=1, device_id=dev, device_id_type=MESH)

    for k in range(1, NLAT):
        greet((b, lax.rem(l + k, NLAT)))
    for k in range(1, NBLK):
        greet((lax.rem(b + k, NBLK), l))
    for side in (east_b, west_b):
        greet((side, lax.rem(l + 1, NLAT)))
        greet((side, lax.rem(l + NLAT - 1, NLAT)))

    def remote(source, target, sent, got, dev):
        return pltpu.make_async_remote_copy(
            src_ref=source, dst_ref=target, send_sem=send_sem.at[sent], recv_sem=recv_sem.at[got],
            device_id=dev, device_id_type=MESH,
        )

    for part, spot, target in ((0, 8, south_v), (2, 7 + ROWS, north_v)):
        for j in range(TILES):
            ice_copy(part, j).wait()
        for first in range(0, CATS, 8):
            size = min(8, CATS - first)
            for j in range(TILES):
                target[pl.ds(first, size), pl.ds(128 * j, 128)] = ice_v[j, pl.ds(first, size), spot, :]

    to_south = remote(south_v, got_north, 6, 6, (b, down))
    to_north = remote(north_v, got_south, 7, 7, (b, up))
    over = remote(north_v, got_north, 10, 6, (NBLK - 1 - b, l))

    def send_rows():
        pl.semaphore_wait(barrier, NLAT - 1 + NBLK - 1 + 4)

        @pl.when(inner_south)
        def _():
            to_south.start()

        @pl.when(inner_north)
        def _():
            to_north.start()

        @pl.when(at_north)
        def _():
            over.start()

    pl.when(behind)(send_rows)

    for i in range(parts):
        wave_copies[i].wait()

        def rows(block, carry):
            first = pl.multiple_of(share * i + block * 8, 8)
            for half in range(2):
                lanes = pl.ds(128 * half, 128)
                total = wave_v[0, pl.ds(first, 8), lanes]
                for f in range(1, FREQ):
                    total = total + wave_v[f, pl.ds(first, 8), lanes] * (f + 1.0)
                sums_v[half, pl.ds(first, 8), :] = total
            return carry

        lax.fori_loop(0, share // 8, rows, 0)

    route_copy.wait()
    route = route_v[...]
    place = 2 * route
    row = lax.broadcasted_iota(jnp.int32, (FLAT, PEERS), 0)
    ordered = jnp.zeros((FLAT, 128), f32)
    for half in range(2):
        chosen = (row == place + half).astype(f32)
        ordered = ordered + jnp.dot(
            chosen, sums_v[half], precision=lax.Precision.HIGHEST, preferred_element_type=f32
        )
    send_v[...] = ordered

    def blk_copy(k):
        peer = lax.rem(b + k, NBLK)
        return pltpu.make_async_remote_copy(
            src_ref=send_v.at[pl.ds(pl.multiple_of(32 * peer, 32), 32), :],
            dst_ref=mid_v.at[pl.ds(pl.multiple_of(32 * b, 32), 32), :],
            send_sem=blk_send.at[k], recv_sem=blk_recv.at[k],
            device_id=(peer, l), device_id_type=MESH,
        )

    def send_waves():
        for k in range(1, NBLK):
            blk_copy(k).start()

    pl.when(behind)(send_waves)
    own = pl.ds(pl.multiple_of(32 * b, 32), 32)
    mid_v[own, :] = send_v[own, :]

    for j in range(TILES):
        for first in range(0, CATS, 8):
            size = min(8, CATS - first)
            for spot in (7, 8 + ROWS):
                ice_v[j, pl.ds(first, size), spot, :] = jnp.zeros((size, 128), f32)

    lane = lax.broadcasted_iota(jnp.int32, (8, 128), 1)
    for g in (0, 3, 1, 2):
        if g == 1:
            for j in range(TILES):
                ice_copy(1, j).wait()
        for tile, target, edge in ((0, west_v, 0), (TILES - 1, east_v, 127)):
            held = jnp.zeros((8, 128), f32)
            for cat in range(CATS):
                shift = (cat + 128 - edge) % 128
                column = ice_v[tile, cat, pl.ds(8 + 8 * g, 8), :]
                held = jnp.where(lane == cat, pltpu.roll(column, shift, 1) if shift else column, held)
            target[pl.ds(8 * g, 8), :] = held

    low = pl.ds(0, 8)
    high = pl.ds(ROWS - 8, 8)
    nw_c, ne_c, sw_c, se_c = (corner_v.at[i] for i in range(4))
    to_east = remote(east_v, got_west, 0, 0, (east_b, l))
    to_west = remote(west_v, got_east, 1, 1, (west_b, l))
    to_ne = remote(east_v.at[high], sw_c, 2, 2, (east_b, up))
    to_nw = remote(west_v.at[high], se_c, 3, 3, (west_b, up))
    to_se = remote(east_v.at[low], nw_c, 4, 4, (east_b, down))
    to_sw = remote(west_v.at[low], ne_c, 5, 5, (west_b, down))
    fold_nw = lax.rem(2 * NBLK - b, NBLK)
    fold_ne = lax.rem(2 * NBLK - 2 - b, NBLK)
    nw_home = jnp.logical_and(at_north, fold_nw == b)
    ne_home = jnp.logical_and(at_north, fold_ne == b)
    nw_away = jnp.logical_and(at_north, fold_nw != b)
    ne_away = jnp.logical_and(at_north, fold_ne != b)
    over_nw = remote(west_v.at[high], nw_c, 8, 4, (fold_nw, l))
    over_ne = remote(east_v.at[high], ne_c, 9, 5, (fold_ne, l))
    def send_columns():
        to_east.start()
        to_west.start()

        @pl.when(inner_north)
        def _():
            to_ne.start()
            to_nw.start()

        @pl.when(inner_south)
        def _():
            to_se.start()
            to_sw.start()

        @pl.when(nw_away)
        def _():
            over_nw.start()

        @pl.when(ne_away)
        def _():
            over_ne.start()

    pl.when(behind)(send_columns)

    @pl.when(nw_home)
    def _():
        corner_v[0] = west_v[high, :]

    @pl.when(ne_home)
    def _():
        corner_v[1] = east_v[high, :]

    @pl.when(at_south)
    def _():
        corner_v[2] = jnp.zeros((8, 128), f32)
        corner_v[3] = jnp.zeros((8, 128), f32)

    shares_copy.wait()
    for g in range(GROUPS):
        for t in range(9):
            weight = shares_v[t, pl.ds(8 * g, 8), :].astype(f32) * (1.0 / 4096.0)
            if t % 3 == 2:
                weight = pltpu.roll(weight, 1, 1)
            elif t % 3 == 0:
                weight = pltpu.roll(weight, COLS - 1, 1)
            weights_v[g, t] = weight

    @pl.when(ahead)
    def _():
        send_rows()
        send_columns()
        send_waves()

    at_first = lane == 0
    at_last = lane == 127
    batch = 10

    def stencil_group(g):
        def stencil(block, carry):
            before = [None] * batch
            held = [None] * batch
            held_right = [None] * batch
            for j in range(TILES + 1):
                if j < TILES:
                    w = [weights_v[g, t, :, pl.ds(128 * j, 128)] for t in range(9)]
                for i in range(batch):
                    cat = block * batch + i
                    if j < TILES:
                        lower = ice_v[j, cat, pl.ds(7 + 8 * g, 8), :]
                        here = ice_v[j, cat, pl.ds(8 + 8 * g, 8), :]
                        upper = ice_v[j, cat, pl.ds(9 + 8 * g, 8), :]
                        centre = w[1] * lower + w[4] * here + w[7] * upper
                        left = w[0] * lower + w[3] * here + w[6] * upper
                        right = w[2] * lower + w[5] * here + w[8] * upper
                        left = pltpu.roll(left, 1, 1)
                        right = pltpu.roll(right, 127, 1)
                    else:
                        right = 0.0
                    if j > 0:
                        moved_ref[cat, pl.ds(8 * g, 8), pl.ds(128 * (j - 1), 128)] = held[i] + jnp.where(
                            at_last, right, held_right[i]
                        )
                    if j < TILES:
                        held[i] = centre + jnp.where(at_first, 0.0 if j == 0 else before[i], left)
                        before[i] = left
                        held_right[i] = right
            return carry

        lax.fori_loop(0, CATS // batch, stencil, 0)

    stencil_group(0)

    for g in (1, 2, 3):
        stencil_group(g)

    for k in range(1, NBLK):
        blk_copy(k).wait_recv()
    for part in range(NLAT):
        for half in range(2):
            turn_v[pl.ds(16 * part + half, 8, stride=2), :] = mid_v[pl.ds(2 * part + half, 8, stride=32), :]

    def lat_copy(k):
        peer = lax.rem(l + k, NLAT)
        return pltpu.make_async_remote_copy(
            src_ref=turn_v.at[pl.ds(pl.multiple_of(16 * peer, 16), 16), :],
            dst_ref=rate_ref.at[pl.ds(pl.multiple_of(16 * l, 16), 16), :],
            send_sem=lat_send.at[k], recv_sem=lat_recv.at[k],
            device_id=(b, peer), device_id_type=MESH,
        )

    for k in range(1, NLAT):
        lat_copy(k).start()
    mine = pl.ds(pl.multiple_of(16 * l, 16), 16)
    rate_ref[mine, :] = turn_v[mine, :]

    to_east.wait()
    to_west.wait()

    @pl.when(inner_north)
    def _():
        to_ne.wait_send()
        to_nw.wait_send()
        to_se.wait_recv()
        to_sw.wait_recv()

    @pl.when(inner_south)
    def _():
        to_se.wait_send()
        to_sw.wait_send()
        to_ne.wait_recv()
        to_nw.wait_recv()

    @pl.when(nw_away)
    def _():
        over_nw.wait()

    @pl.when(ne_away)
    def _():
        over_ne.wait()

    top_west = jnp.where(at_north, corner_v[0, pl.ds(7, 1), :], corner_v[0, pl.ds(0, 1), :])
    top_east = jnp.where(at_north, corner_v[1, pl.ds(7, 1), :], corner_v[1, pl.ds(0, 1), :])
    for source, target, lower, upper, t, spot in (
        (got_west, west_h, corner_v[2, pl.ds(7, 1), :], top_west, 0, 0),
        (got_east, east_h, corner_v[3, pl.ds(7, 1), :], top_east, 2, 127),
    ):
        target[pl.ds(8, ROWS), :] = source[...]
        target[pl.ds(7, 1), :] = lower
        target[pl.ds(8 + ROWS, 1), :] = upper
        tile = pl.ds(0 if spot == 0 else COLS - 128, 128)
        for g in range(GROUPS):
            rows = pl.ds(8 * g, 8)
            total = jnp.zeros((8, 128), f32)
            for dy in range(3):
                weight = shares_v[3 * dy + t, rows, tile].astype(f32) * (1.0 / 4096.0)
                total = total + weight[:, spot : spot + 1] * target[pl.ds(7 + dy + 8 * g, 8), :]
            source[rows, :] = total

    for g in range(GROUPS):
        rows = pl.ds(8 * g, 8)
        west = got_west[rows, :]
        east = got_east[rows, :]
        for cat in range(CATS):
            first = pltpu.roll(west, 128 - cat, 1) if cat else west
            moved_ref[cat, rows, pl.ds(0, 128)] += jnp.where(at_first, first, 0.0)
            last = pltpu.roll(east, 127 - cat, 1)
            moved_ref[cat, rows, pl.ds(COLS - 128, 128)] += jnp.where(at_last, last, 0.0)

    weld_copy.wait()
    cover_copy.wait()
    for g in range(GROUPS):
        rows = pl.ds(8 * g, 8)
        weld_v[rows, :] = weld_v[rows, :] * (covered_rows(cover_v[...], g) * 0.06)

    def weld_part(part, carry):
        group = part // NCAT
        n = part - NCAT * group
        rows = pl.ds(pl.multiple_of(8 * group, 8), 8)
        for j in range(TILES):
            lanes = pl.ds(128 * j, 128)
            area = [moved_ref[NFSD * n + k, rows, lanes] for k in range(NFSD)]
            grown = welded(area, weld_v[rows, lanes])
            for k in range(NFSD):
                moved_ref[NFSD * n + k, rows, lanes] = grown[k]
        return carry

    lax.fori_loop(NCAT, 3 * NCAT, weld_part, 0)

    @pl.when(inner_south)
    def _():
        to_south.wait_send()
        to_north.wait_recv()

    @pl.when(at_south)
    def _():
        got_south[...] = jnp.zeros_like(got_south)

    @pl.when(inner_north)
    def _():
        to_north.wait_send()
        to_south.wait_recv()

    @pl.when(at_north)
    def _():
        over.wait()
        first = lax.broadcasted_iota(jnp.int32, (128, 128), 0)
        second = lax.broadcasted_iota(jnp.int32, (128, 128), 1)
        mirror = (first + second == 127).astype(f32)
        for j in range(TILES // 2):
            one = pl.ds(128 * j, 128)
            other = pl.ds(128 * (TILES - 1 - j), 128)
            turned = [
                jnp.dot(got_north[:, lanes], mirror, precision=lax.Precision.HIGHEST, preferred_element_type=f32)
                for lanes in (other, one)
            ]
            got_north[:, one] = turned[0]
            got_north[:, other] = turned[1]

    place_x = lax.broadcasted_iota(jnp.int32, (1, COLS), 1)
    for source, t, spot in ((got_south, 0, 0), (got_north, 6, ROWS - 1)):
        weight = [shares_v[t + dx, pl.ds(spot, 1), :].astype(f32) * (1.0 / 4096.0) for dx in range(3)]
        weight[0] = jnp.where(place_x == 0, 0.0, weight[0])
        weight[2] = jnp.where(place_x == COLS - 1, 0.0, weight[2])
        for first in range(0, CATS, 8):
            size = min(8, CATS - first)
            line = source[pl.ds(first, size), :]
            added = weight[1] * line + weight[0] * pltpu.roll(line, 1, 1) + weight[2] * pltpu.roll(line, COLS - 1, 1)
            for j in range(TILES):
                lanes = pl.ds(128 * j, 128)
                moved_ref[pl.ds(first, size), spot, lanes] += added[:, 128 * j : 128 * (j + 1)]

    lax.fori_loop(0, NCAT, weld_part, 0)
    lax.fori_loop(3 * NCAT, 4 * NCAT, weld_part, 0)

    for k in range(1, NBLK):
        blk_copy(k).wait_send()
    for k in range(1, NLAT):
        lat_copy(k).wait()


def front(route, wave, ice, shares, weld, cover):
    f32 = jnp.float32
    dma = pltpu.SemaphoreType.DMA
    return pl.pallas_call(
        front_kernel,
        name="front",
        out_shape=(pltpu.VMEM((CATS, ROWS, COLS), f32), pltpu.VMEM((FLAT, 128), f32)),
        in_specs=[any_spec()] * 6,
        out_specs=(vmem_spec(), vmem_spec()),
        scratch_shapes=[
            pltpu.VMEM((FREQ, PEERS, 256), f32),
            pltpu.VMEM((2, PEERS, 128), f32),
            pltpu.VMEM((FLAT, 128), f32),
            pltpu.VMEM((FLAT, 128), f32),
            pltpu.VMEM((FLAT, 128), f32),
            pltpu.VMEM((TILES, CATS, ROWS + 16, 128), f32),
            pltpu.VMEM((9, ROWS, COLS), jnp.int32),
            pltpu.VMEM((GROUPS, 9, 8, COLS), f32),
            pltpu.VMEM((CATS, COLS), f32),
            pltpu.VMEM((CATS, COLS), f32),
            pltpu.VMEM((CATS, COLS), f32),
            pltpu.VMEM((CATS, COLS), f32),
            pltpu.VMEM((ROWS, 128), f32),
            pltpu.VMEM((ROWS, 128), f32),
            pltpu.VMEM((ROWS, 128), f32),
            pltpu.VMEM((ROWS, 128), f32),
            pltpu.VMEM((4, 8, 128), f32),
            pltpu.VMEM((ROWS + 16, 128), f32),
            pltpu.VMEM((ROWS + 16, 128), f32),
            pltpu.VMEM((ROWS, COLS), f32),
            pltpu.VMEM((1, ROWS), jnp.int32),
            pltpu.VMEM((1, PEERS), jnp.int32),
            dma((2,)),
            dma,
            dma((4,)),
            dma((3, TILES)),
            dma,
            dma((NLAT,)),
            dma((NLAT,)),
            dma((NBLK,)),
            dma((NBLK,)),
            dma((11,)),
            dma((8,)),
        ],
        compiler_params=pltpu.CompilerParams(
            collective_id=0, has_side_effects=True, vmem_limit_bytes=FRONT_LIMIT
        ),
    )(*(pltpu.with_memory_space_constraint(x, pltpu.HBM) for x in (route, wave, ice, shares, weld, cover)))


def cracked(grown, crack):
    result = [None] * NFSD
    above = None
    for k in range(NFSD - 1, -1, -1):
        scaled = crack * grown[k]
        value = grown[k] - scaled * float(k) if k > 0 else grown[k]
        if above is not None:
            value = value + above
        above = scaled if above is None else above + scaled
        result[k] = value
    return result


def back_kernel(welded_ref, cover_ref, rate_ref, out_hbm, out_v, crack_v, out_sem):
    def out_copy(part):
        group = part // NCAT
        cats = pl.ds(NFSD * (part - NCAT * group), NFSD)
        rows = pl.ds(pl.multiple_of(8 * group, 8), 8)
        return pltpu.make_async_copy(out_v.at[cats, rows, :], out_hbm.at[cats, rows, :], out_sem.at[part])

    def chunk(part, carry):
        group = part // NCAT
        n = part - NCAT * group
        rows = pl.ds(pl.multiple_of(8 * group, 8), 8)
        thick = 1.0 / (1.0 + 0.5 * jnp.full((8, 128), n, jnp.int32).astype(jnp.float32))
        for j in range(TILES):
            lanes = pl.ds(128 * j, 128)
            grown = [welded_ref[NFSD * n + k, rows, lanes] for k in range(NFSD)]
            result = cracked(grown, crack_v[rows, lanes] * thick)
            for k in range(NFSD):
                out_v[NFSD * n + k, rows, lanes] = result[k]
        out_copy(part).start()
        return carry

    for g in range(GROUPS):
        rows = pl.ds(8 * g, 8)
        covered = covered_rows(cover_ref[...], g)
        for j in range(TILES):
            for half in range(2):
                crack_v[pl.ds(8 * g + 4 * half, 4), pl.ds(128 * j, 128)] = rate_ref[
                    pl.ds(16 * (j // 2) + 4 * g + 2 * half + j % 2, 4, stride=64), :
                ]
        crack_v[rows, :] = crack_v[rows, :] * covered * (0.1 / 11.0 / FREQ)
        lax.fori_loop(g * NCAT, (g + 1) * NCAT, chunk, 0)

    for part in range(GROUPS * NCAT):
        out_copy(part).wait()


def back(grown, cover, rate):
    f32 = jnp.float32
    return pl.pallas_call(
        back_kernel,
        name="back",
        out_shape=jax.ShapeDtypeStruct((CATS, ROWS, COLS), f32),
        in_specs=[vmem_spec()] * 3,
        out_specs=any_spec(),
        scratch_shapes=[
            pltpu.VMEM((CATS, ROWS, COLS), f32),
            pltpu.VMEM((ROWS, COLS), f32),
            pltpu.SemaphoreType.DMA((GROUPS * NCAT,)),
        ],
        compiler_params=pltpu.CompilerParams(vmem_limit_bytes=BACK_LIMIT),
    )(grown, cover, rate)


def on_device(ice_area, departure_weights, weld_rate, ice_cover, wave_ocean, ocean_route):
    ice = ice_area.reshape(CATS, ROWS, COLS)
    cover = ice_cover.reshape(1, ROWS)
    grown, rate = front(ocean_route, wave_ocean[0], ice, departure_weights, weld_rate, cover)
    out = back(grown, cover, rate)
    return out.reshape(ice_area.shape)


def solution(mesh):
    return jax.shard_map(
        on_device,
        mesh=mesh,
        in_specs=(
            P(None, None, "lat", "blk"),
            P(None, "lat", "blk"),
            P("lat", "blk"),
            P("lat", "blk"),
            P(("blk", "lat"), None, None, None),
            P(("blk", "lat"), None),
        ),
        out_specs=P(None, None, "lat", "blk"),
        check_vma=False,
    )
```
